32 devices in a mesh: groups: 2 (over y), dp: 4 (over z), fsdp: 4 (over x, core).
Axes of the slice: x: 2, y: 2, z: 4, core: 2. Of those that a mesh axis runs over, the one named last changes fastest.
Arguments:
- tokens: bfloat16 [8192, 4096], P(('groups', 'dp', 'fsdp')), parts along dimension 0, may hold values from -6 to 6
- key_value_weight: bfloat16 [4096, 2048], P('fsdp'), may hold values from -0.09375 to 0.09375
- adapter_down_maps: bfloat16 [8, 32, 4096], P(('groups', 'fsdp')), parts along dimension 0, may hold values from -0.09375 to 0.09375
- adapter_up_maps: bfloat16 [8, 32, 1024], P(('groups', 'fsdp')), parts along dimension 0, may hold values from -0.75 to 0.75
- counts: int32 [8, 4], P(('groups', 'dp')), parts along dimension 0, may hold values from 1 to 512, 1024 in all within a row
- tenant_slot_index: int32 [8], P('groups'), parts along dimension 0, may hold values from 0 to 3, each once
- cotangent: bfloat16 [8192, 2048], P(('groups', 'dp', 'fsdp')), parts along dimension 0, may hold values from -6 to 6
Outputs:
- key_value_output: bfloat16 [8192, 2048], P(('groups', 'dp', 'fsdp')), parts along dimension 0
- grad_x: bfloat16 [8192, 4096], P(('groups', 'dp', 'fsdp')), parts along dimension 0
- grad_down: float32 [8, 32, 4096], P(('groups', 'fsdp')), parts along dimension 0
- grad_up: float32 [8, 32, 1024], P(('groups', 'fsdp')), parts along dimension 0
The draws below stay inside these ranges and needn't reach their ends.
There are 2 independent parts, one for each index of `groups`. The reference program is written for one: setup_inputs(seed, part) draws one part's arguments, and reference() takes and returns one part's arrays. A program takes and returns all parts, laid end to end along the dimension named above; an argument that names none is the same for every part. Nothing has to cross between parts.
Inputs may be any that keep to these rules, and one draw needn't show every extreme that they name: Each row gives the token counts of the 4 tenants in one data group, in the order in which their tokens stand, and sums to 1024; every tenant has a token in every group and some tenant holds exactly 512 tokens of each group. `tenant_slot_index`: A permutation of the slots.
All inputs are finite; a program needn't handle non-finite values.
Results may differ from the reference program's by a relative error of at most 0.0095.
Values may be sent and summed in bfloat16 or wider, within the bound.
No kernel may reach another device: no remote copies, remote signals or barrier semaphores. Data moves between devices by JAX's collectives and lax.ppermute only.
A program may use at most 128 MiB of HBM per device.

```python
import math
import jax
import jax.numpy as jnp
import numpy as np
from jax import lax

MODEL_WIDTH = 4096
KEY_VALUE_WIDTH = 1024
ADAPTER_RANK = 16
TOK_DEV = 256
TENANT_COUNT = 4
GROUP_TOKENS = 1024
TOKENS = 4096
N_DP = 4


def levels(stream_key, shape, cuts, least, high):
    loudness = 1.0
    for axis_at, blocks in cuts:
        steps = jax.random.uniform(jax.random.fold_in(jax.random.fold_in(stream_key, 6), axis_at), (blocks,), jnp.float32, least / len(cuts), high / len(cuts))
        loudness = loudness * jnp.repeat(jnp.exp(steps), shape[axis_at] // blocks).reshape((-1,) + (1,) * (len(shape) - 1 - axis_at))
    return loudness


def split_up(count, total, limit, slope):
    loads = [(1 << 20) // math.isqrt(rank ** slope) + 1 for rank in range(2, count + 1)]
    surplus, holding = total - limit - (count - 1), [1] * (count - 1)
    while surplus > 0:
        movable = [i for i in range(count - 1) if holding[i] < limit]
        mass, budget = sum([loads[i] for i in movable]), surplus
        for i in movable:
            extra = min(limit - holding[i], max(1, budget * loads[i] // mass), surplus)
            holding[i] = holding[i] + extra
            surplus = surplus - extra
    return np.array([limit] + holding)


def ragged_sizes(key, amount, total, bound, lean):
    if amount == 2:
        one = jax.random.randint(key, (), max(1, total - bound), min(bound, total - 1) + 1)
        return jnp.stack([one, total - one])
    tallies = jnp.asarray(split_up(amount, total, bound, lean), jnp.int32)
    couples = (amount - 1) // 2
    giver, sink = tallies[1:1 + 2 * couples:2], tallies[2:2 + 2 * couples:2]
    margin = jnp.minimum(giver - 1, bound - sink)
    shifted = jax.random.randint(jax.random.fold_in(key, 1), (couples,), 0, 1 << 20) % (margin + 1)
    tallies = tallies.at[1:1 + 2 * couples:2].set(giver - shifted).at[2:2 + 2 * couples:2].set(sink + shifted)
    return tallies[jax.random.permutation(jax.random.fold_in(key, 2), amount)]


def scatter_about(rng, dims, width, bound, cuts=(), held_as=jnp.bfloat16):
    factor_of = levels(rng, dims, cuts, -0.22, 0.18) if cuts else 1.0
    array = jax.random.normal(rng, dims, jnp.float32) * width * factor_of
    return jnp.minimum(jnp.maximum(array, -bound), bound).astype(held_as)


def setup_inputs(seed: int = 0, part: int = 0) -> dict:
    arg_keys = jax.random.split(jax.random.key(seed), 8)
    part_keys = jax.random.split(jax.random.fold_in(arg_keys[7], part), 8)
    return {
        "tokens": scatter_about(part_keys[0], (TOKENS, MODEL_WIDTH), 1.0, 6.0, ((0, 16),)),
        "key_value_weight": scatter_about(arg_keys[1], (MODEL_WIDTH, 2 * KEY_VALUE_WIDTH), MODEL_WIDTH ** -0.5, 0.09375, ((0, 4),)),
        "adapter_down_maps": scatter_about(part_keys[2], (TENANT_COUNT, 2 * ADAPTER_RANK, MODEL_WIDTH), MODEL_WIDTH ** -0.5, 0.09375, ((0, 4),)),
        "adapter_up_maps": scatter_about(part_keys[3], (TENANT_COUNT, 2 * ADAPTER_RANK, KEY_VALUE_WIDTH), (4 * ADAPTER_RANK) ** -0.5, 0.75, ((0, 4),)),
        "counts": jax.vmap(lambda own: ragged_sizes(own, TENANT_COUNT, GROUP_TOKENS, GROUP_TOKENS // 2, 2))(jax.random.split(part_keys[4], N_DP)).reshape((N_DP, TENANT_COUNT)).astype(jnp.int32),
        "tenant_slot_index": jax.random.permutation(part_keys[5], TENANT_COUNT).astype(jnp.int32),
        "cotangent": scatter_about(part_keys[6], (TOKENS, 2 * KEY_VALUE_WIDTH), 1.0, 6.0, ((0, 16),)),
    }


ADAPTER_SCALE = 2.0


def token_slots(counts, tenant_slot_index):
    positions = jnp.arange(TOKENS, dtype=jnp.int32)
    group_ids = positions // GROUP_TOKENS
    inner_pos = positions % GROUP_TOKENS
    tenant_ends = jnp.cumsum(counts, axis=1).astype(jnp.int32)[group_ids]
    tenant = jnp.sum((inner_pos[:, None] >= tenant_ends).astype(jnp.int32), axis=1).astype(jnp.int32)
    return tenant_slot_index[tenant].astype(jnp.int32)


def rounded(value):
    return lax.optimization_barrier(value.astype(jnp.bfloat16)).astype(jnp.float32)


def reference(tokens, key_value_weight, adapter_down_maps, adapter_up_maps, counts, tenant_slot_index, cotangent):
    slot_ids = token_slots(counts, tenant_slot_index)
    select = slot_ids[:, None] == jnp.arange(TENANT_COUNT, dtype=jnp.int32)[None, :]
    frozen_output = jnp.dot(tokens, key_value_weight, preferred_element_type=jnp.float32)
    flattened_down = adapter_down_maps.reshape(TENANT_COUNT * 2 * ADAPTER_RANK, MODEL_WIDTH)
    projected = jnp.dot(tokens, flattened_down.T, preferred_element_type=jnp.float32).reshape(TOKENS, TENANT_COUNT, 2 * ADAPTER_RANK)
    low_rank = jnp.sum(jnp.where(select[:, :, None], projected, 0.0), axis=1).astype(jnp.bfloat16)
    spread = jnp.where(select[:, :, None], low_rank[:, None, :], jnp.zeros((), jnp.bfloat16))
    widened_keys = spread[:, :, :ADAPTER_RANK].reshape(TOKENS, TENANT_COUNT * ADAPTER_RANK)
    spread_vals = spread[:, :, ADAPTER_RANK:].reshape(TOKENS, TENANT_COUNT * ADAPTER_RANK)
    key_up_maps = adapter_up_maps[:, :ADAPTER_RANK, :].reshape(TENANT_COUNT * ADAPTER_RANK, KEY_VALUE_WIDTH)
    value_up_maps = adapter_up_maps[:, ADAPTER_RANK:, :].reshape(TENANT_COUNT * ADAPTER_RANK, KEY_VALUE_WIDTH)
    adapter_update = jnp.concatenate([jnp.dot(widened_keys, key_up_maps, preferred_element_type=jnp.float32),
                                  jnp.dot(spread_vals, value_up_maps, preferred_element_type=jnp.float32)], axis=1)
    key_value_output = (frozen_output + ADAPTER_SCALE * adapter_update).astype(jnp.bfloat16)
    back_keys = jnp.dot(cotangent[:, :KEY_VALUE_WIDTH], key_up_maps.T, preferred_element_type=jnp.float32).reshape(TOKENS, TENANT_COUNT, ADAPTER_RANK)
    back_vals = jnp.dot(cotangent[:, KEY_VALUE_WIDTH:], value_up_maps.T, preferred_element_type=jnp.float32).reshape(TOKENS, TENANT_COUNT, ADAPTER_RANK)
    back_all = jnp.concatenate([back_keys, back_vals], axis=2)
    grad_low = (ADAPTER_SCALE * jnp.sum(jnp.where(select[:, :, None], back_all, 0.0), axis=1)).astype(jnp.bfloat16)
    spread_grad = jnp.where(select[:, :, None], grad_low[:, None, :], jnp.zeros((), jnp.bfloat16)).reshape(TOKENS, TENANT_COUNT * 2 * ADAPTER_RANK)
    grad_x = (jnp.dot(cotangent, key_value_weight.T, preferred_element_type=jnp.float32)
              + jnp.dot(spread_grad, flattened_down, preferred_element_type=jnp.float32)).astype(jnp.bfloat16)
    blocks = TOKENS // TOK_DEV
    pieces = (spread_grad.reshape(blocks, TOK_DEV, TENANT_COUNT * 2 * ADAPTER_RANK), tokens.reshape(blocks, TOK_DEV, MODEL_WIDTH),
              widened_keys.reshape(blocks, TOK_DEV, TENANT_COUNT * ADAPTER_RANK), spread_vals.reshape(blocks, TOK_DEV, TENANT_COUNT * ADAPTER_RANK),
              cotangent.reshape(blocks, TOK_DEV, 2 * KEY_VALUE_WIDTH))

    def accumulate(totals, piece_set):
        grad_piece, token_piece, keys_piece, vals_piece, cot_piece = piece_set
        down_term = jnp.dot(grad_piece.T, token_piece, preferred_element_type=jnp.float32).reshape(TENANT_COUNT, 2 * ADAPTER_RANK, MODEL_WIDTH)
        keys_term = ADAPTER_SCALE * jnp.dot(keys_piece.T, cot_piece[:, :KEY_VALUE_WIDTH], preferred_element_type=jnp.float32)
        vals_term = ADAPTER_SCALE * jnp.dot(vals_piece.T, cot_piece[:, KEY_VALUE_WIDTH:], preferred_element_type=jnp.float32)
        up_term = jnp.concatenate([keys_term.reshape(TENANT_COUNT, ADAPTER_RANK, KEY_VALUE_WIDTH), vals_term.reshape(TENANT_COUNT, ADAPTER_RANK, KEY_VALUE_WIDTH)], axis=1)
        return (totals[0] + rounded(down_term), totals[1] + rounded(up_term)), None

    start = (jnp.zeros((TENANT_COUNT, 2 * ADAPTER_RANK, MODEL_WIDTH), jnp.float32), jnp.zeros((TENANT_COUNT, 2 * ADAPTER_RANK, KEY_VALUE_WIDTH), jnp.float32))
    sums, unused = lax.scan(accumulate, start, pieces)
    return key_value_output, grad_x, sums[0], sums[1]
```

```python
import functools

import jax
import jax.numpy as jnp
from jax import lax
from jax.experimental import pallas as pl
from jax.experimental.pallas import tpu as pltpu
from jax.sharding import PartitionSpec as P

ADAPTER_SCALE = 2.0
F32 = jnp.float32
BF16 = jnp.bfloat16
CONTRACT_LAST = (((1,), (1,)), ((), ()))
CONTRACT_FIRST = (((0,), (0,)), ((), ()))


def dot(a, b, dims=(((1,), (0,)), ((), ()))):
    return lax.dot_general(a, b, dims, preferred_element_type=F32)


def low_rank_kernel(slots, rank2, width, kv, bounds, tok, cot, *refs):
    packs = refs[:slots]
    spread_low, spread_grad, down_cat, up_cat, keep, send = refs[slots:]
    rows = tok.shape[0]
    for r in range(slots):
        down_cat[pl.ds(r * rank2, rank2), :] = packs[r][:, :width]
        up_cat[pl.ds(r * rank2, rank2), :] = packs[r][:, width:]
    pos = lax.broadcasted_iota(jnp.int32, (rows, slots * rank2), 0)
    col = lax.broadcasted_iota(jnp.int32, (rows, slots * rank2), 1)
    slot = col // rank2
    is_key = (col % rank2) < (rank2 // 2)
    mask = jnp.zeros((rows, slots * rank2), jnp.bool_)
    for r in range(slots):
        inside = (pos >= bounds[0, r]) & (pos < bounds[1, r])
        mask = mask | ((slot == r) & inside)
    low = jnp.where(mask, dot(tok[...], down_cat[...], CONTRACT_LAST), 0.0).astype(BF16)
    spread_low[...] = low
    back_keys = dot(cot[:, :kv], up_cat[...], CONTRACT_LAST)
    back_vals = dot(cot[:, kv:], up_cat[...], CONTRACT_LAST)
    back = ADAPTER_SCALE * jnp.where(is_key, back_keys, back_vals)
    grad = jnp.where(mask, back, 0.0).astype(BF16)
    spread_grad[...] = grad

    def put(r, cols, value):
        ref = keep if r % 2 == 0 else send
        ref[r // 2, :, cols] = value.astype(BF16)

    step = 1024
    for start in range(0, width, step):
        part = dot(grad, tok[:, start : start + step], CONTRACT_FIRST)
        for r in range(slots):
            put(r, slice(start, start + step), part[r * rank2 : (r + 1) * rank2])
    part_keys = ADAPTER_SCALE * dot(low, cot[:, :kv], CONTRACT_FIRST)
    part_vals = ADAPTER_SCALE * dot(low, cot[:, kv:], CONTRACT_FIRST)
    row = lax.broadcasted_iota(jnp.int32, (slots * rank2, kv), 0)
    part = jnp.where((row % rank2) < (rank2 // 2), part_keys, part_vals)
    for r in range(slots):
        put(r, slice(width, width + kv), part[r * rank2 : (r + 1) * rank2])


def low_rank_call(bounds, tok, cot, packs, width, kv):
    slots = len(packs)
    rank2 = packs[0].shape[0]
    rows = tok.shape[0]
    vm = pl.BlockSpec(memory_space=pltpu.VMEM)
    half = jax.ShapeDtypeStruct((slots // 2, rank2, width + kv), BF16)
    return pl.pallas_call(
        functools.partial(low_rank_kernel, slots, rank2, width, kv),
        out_shape=(
            jax.ShapeDtypeStruct((rows, slots * rank2), BF16),
            jax.ShapeDtypeStruct((rows, slots * rank2), BF16),
            jax.ShapeDtypeStruct((slots * rank2, width), BF16),
            jax.ShapeDtypeStruct((slots * rank2, kv), BF16),
            half,
            half,
        ),
        in_specs=[pl.BlockSpec(memory_space=pltpu.SMEM)] + [vm] * (2 + slots),
        out_specs=(vm,) * 6,
        compiler_params=pltpu.CompilerParams(vmem_limit_bytes=40 << 20),
        cost_estimate=pl.CostEstimate(
            flops=12 * rows * width * slots * rank2, bytes_accessed=8 << 20, transcendentals=0
        ),
        name="low_rank",
    )(bounds, tok, cot, *packs)


def matmul_kernel(layout, rank2, kv, first, last, *refs):
    refs = list(refs)
    refs.pop(0)
    tok, cot, low, grad, down, up = (refs.pop(0) for _ in range(6))
    sources = [[refs.pop(0) for _ in range(count)] for count, _, _ in layout]
    if not first:
        acc_in = refs.pop(0)
        refs.pop(0)
    out, gx = refs.pop(0), refs.pop(0)
    acc = refs.pop(0) if last else out
    step = pl.program_id(0)
    total = pl.num_programs(0)

    @pl.when(step == 0)
    def _():
        if first:
            col = lax.broadcasted_iota(jnp.int32, low.shape, 1)
            is_key = (col % rank2) < (rank2 // 2)
            zero = jnp.zeros(low.shape, BF16)
            low_keys = jnp.where(is_key, low[...], zero)
            low_vals = jnp.where(is_key, zero, low[...])
            acc[:, :kv] = ADAPTER_SCALE * dot(low_keys, up[...])
            acc[:, kv:] = ADAPTER_SCALE * dot(low_vals, up[...])
        else:
            acc[...] = acc_in[...]

    for (_, offset, blocks), chunks in zip(layout, sources):

        @pl.when((step >= offset) & (step < offset + blocks))
        def _():
            back = dot(grad[...], down[...])
            start = 0
            for chunk in chunks:
                cols = slice(start, start + chunk.shape[1])
                start += chunk.shape[1]
                weight = chunk[...]
                acc[:, cols] += dot(tok[...], weight)
                back += dot(cot[:, cols], weight, CONTRACT_LAST)
            gx[...] = back.astype(BF16)

    if last:

        @pl.when(step == total - 1)
        def _():
            out[...] = acc[...].astype(BF16)


def matmul_call(table, tok, cot, low, grad, down, up, sources, block, prev, last, name):
    rows, width = tok.shape
    cols = cot.shape[1]
    kv = up.shape[1]
    slot_rows = down.shape[0]
    layout, specs, arrays, offset = [], [], [], 0
    for chunks in sources:
        blocks = chunks[0].shape[0] // block
        layout.append((len(chunks), offset, blocks))
        for chunk in chunks:
            index = functools.partial(
                lambda o, n, s, t: (jnp.clip(s - o, 0, n - 1), 0), offset, blocks
            )
            specs.append(pl.BlockSpec((block, chunk.shape[1]), index))
            arrays.append(chunk)
        offset += blocks
    fixed = lambda s, t: (0, 0)
    moving = lambda s, t: (0, t[s])
    in_specs = [
        pl.BlockSpec((rows, block), moving),
        pl.BlockSpec(cot.shape, fixed),
        pl.BlockSpec(low.shape, fixed),
        pl.BlockSpec(grad.shape, fixed),
        pl.BlockSpec((slot_rows, block), moving),
        pl.BlockSpec(up.shape, fixed),
    ] + specs
    args = [table, tok, cot, low, grad, down, up] + arrays
    first = prev is None
    aliases = {}
    if not first:
        in_specs += [
            pl.BlockSpec((rows, cols), fixed),
            pl.BlockSpec(memory_space=pl.ANY),
        ]
        args += list(prev)
        aliases = {len(args) - 1: 1}
        if not last:
            aliases[len(args) - 2] = 0
    rank2 = ADAPTER_ROWS
    return pl.pallas_call(
        functools.partial(matmul_kernel, tuple(layout), rank2, kv, first, last),
        out_shape=(
            jax.ShapeDtypeStruct((rows, cols), BF16 if last else F32),
            jax.ShapeDtypeStruct((rows, width), BF16),
        ),
        grid_spec=pltpu.PrefetchScalarGridSpec(
            num_scalar_prefetch=1,
            grid=(offset,),
            in_specs=in_specs,
            out_specs=(
                pl.BlockSpec((rows, cols), fixed),
                pl.BlockSpec((rows, block), moving),
            ),
            scratch_shapes=[pltpu.VMEM((rows, cols), F32)] if last else [],
        ),
        input_output_aliases=aliases,
        compiler_params=pltpu.CompilerParams(
            vmem_limit_bytes=40 << 20, dimension_semantics=("arbitrary",)
        ),
        cost_estimate=pl.CostEstimate(
            flops=4 * rows * block * offset * cols,
            bytes_accessed=2 * block * offset * cols,
            transcendentals=0,
        ),
        name=name,
    )(*args)


ADAPTER_ROWS = 32


def xor_swap(value, axis, size, bit):
    return lax.ppermute(value, axis, [(i, i ^ bit) for i in range(size)])


def per_device(
    n_groups,
    n_dp,
    n_fsdp,
    tokens,
    key_value_weight,
    adapter_down_maps,
    adapter_up_maps,
    counts,
    tenant_slot_index,
    cotangent,
):
    rows, width = tokens.shape
    slots = tenant_slot_index.shape[0]
    kv = adapter_up_maps.shape[2]
    shard = key_value_weight.shape[0]
    cols = key_value_weight.shape[1]
    me = lax.axis_index("fsdp")
    group = lax.axis_index("groups")
    data = lax.axis_index("dp")
    swap = lambda value, bit: xor_swap(value, "fsdp", n_fsdp, bit)
    high_bits = [b for b in range(2, n_fsdp, 2)]

    pack = jnp.concatenate([adapter_down_maps[0], adapter_up_maps[0]], axis=1)
    packs = {0: pack}
    for bit in high_bits:
        packs[bit] = swap(pack, bit)
    for bit in [0] + high_bits:
        packs[bit + 1] = swap(packs[bit], 1)

    quartered = n_groups == 2 and n_dp % 2 == 0 and shard % 1024 == 0
    pieces = [[(0, 0, [key_value_weight])], [(1, 0, [swap(key_value_weight, 1)])]]
    if quartered:
        block = shard // 4
        parity = data % 2
        pos = lambda a, b: (((group + a) % 2) * 2 + (parity + b) % 2) * block
        mine = lax.dynamic_slice_in_dim(key_value_weight, pos(0, 0), block, 0)
        chunks = 2
        span = cols // chunks
        sent = [mine[:, i * span : (i + 1) * span] for i in range(chunks)]
        stages = []
        for bit in high_bits:
            direct = [swap(c, bit) for c in sent]
            via_y = [xor_swap(c, "groups", n_groups, 1) for c in direct]
            via_z = [xor_swap(c, "dp", n_dp, 1) for c in direct]
            diagonal = [
                xor_swap(via_z[0], "groups", n_groups, 1),
                xor_swap(via_y[1], "dp", n_dp, 1),
            ]
            stages.append([(bit, pos(0, 0), direct)])
            stages.append([(bit, pos(1, 0), via_y), (bit, pos(0, 1), via_z)])
            stages.append([(bit, pos(1, 1), diagonal)])
        for stage in stages:
            both = []
            for rel, at, parts in stage:
                both.append((rel, at, parts))
                both.append((rel + 1, at, [swap(c, 1) for c in parts]))
            pieces.append(both)
    else:
        block = min(shard, 256)
        for bit in high_bits:
            direct = swap(key_value_weight, bit)
            pieces.append([(bit, 0, [direct]), (bit + 1, 0, [swap(direct, 1)])])
    calls = [pieces[0] + pieces[1]]
    rest = pieces[2:]
    if len(rest) > 3:
        rest = [sum(rest, [])]
    calls += rest

    ends = jnp.cumsum(counts[0]) - me * rows
    starts = ends - counts[0]
    rel_slot = jnp.bitwise_xor(tenant_slot_index, me)
    hit = rel_slot[None, :] == lax.iota(jnp.int32, slots)[:, None]
    bounds = jnp.stack(
        [
            jnp.sum(jnp.where(hit, starts[None, :], 0), axis=1),
            jnp.sum(jnp.where(hit, ends[None, :], 0), axis=1),
        ]
    ).astype(jnp.int32)
    low, grad, down_cat, up_cat, keep, send = low_rank_call(
        bounds, tokens, cotangent, [packs[r] for r in range(slots)], width, kv
    )

    add = lambda a, b: (a.astype(F32) + b.astype(F32)).astype(BF16)
    total = add(keep, swap(send, 1))
    bit = 2
    while bit < n_fsdp:
        pairs = total.reshape((total.shape[0] // 2, 2) + total.shape[1:])
        total = add(pairs[:, 0], swap(pairs[:, 1], bit))
        bit *= 2
    total = total[0]
    bit, trail = 1, []
    while bit < n_dp:
        if bit * 2 < n_dp and total.shape[0] % 32 == 0:
            half = total.shape[0] // 2
            upper = (data // bit) % 2 == 1
            mine = jnp.where(upper, total[half:], total[:half])
            other = jnp.where(upper, total[:half], total[half:])
            total = add(mine, xor_swap(other, "dp", n_dp, bit))
            trail.append((bit, upper))
        else:
            total = add(total, xor_swap(total, "dp", n_dp, bit))
        bit *= 2
    for bit, upper in reversed(trail):
        other = xor_swap(total, "dp", n_dp, bit)
        total = jnp.concatenate(
            [jnp.where(upper, other, total), jnp.where(upper, total, other)], axis=0
        )
    total = total.astype(F32)
    grad_down, grad_up = total[None, :, :width], total[None, :, width:]

    prev = None
    per_shard = shard // block
    for number, call in enumerate(calls):
        table, sources = [], []
        for rel, at, parts in call:
            base = jnp.bitwise_xor(me, rel) * per_shard + at // block
            table += [base + i for i in range(parts[0].shape[0] // block)]
            sources.append(parts)
        prev = matmul_call(
            jnp.stack(table).astype(jnp.int32),
            tokens,
            cotangent,
            low,
            grad,
            down_cat,
            up_cat,
            sources,
            block,
            prev,
            number == len(calls) - 1,
            f"matmul_{number}",
        )
    return prev[0], prev[1], grad_down, grad_up


def solution(mesh):
    in_specs = (
        P(("groups", "dp", "fsdp"), None),
        P("fsdp", None),
        P(("groups", "fsdp"), None, None),
        P(("groups", "fsdp"), None, None),
        P(("groups", "dp"), None),
        P("groups"),
        P(("groups", "dp", "fsdp"), None),
    )
    out_specs = (
        P(("groups", "dp", "fsdp"), None),
        P(("groups", "dp", "fsdp"), None),
        P(("groups", "fsdp"), None, None),
        P(("groups", "fsdp"), None, None),
    )
    body = functools.partial(
        per_device, mesh.shape["groups"], mesh.shape["dp"], mesh.shape["fsdp"]
    )
    return jax.shard_map(
        body, mesh=mesh, in_specs=in_specs, out_specs=out_specs, check_vma=False
    )
```

```python
import functools

import jax
import jax.numpy as jnp
from jax import lax
from jax.experimental import pallas as pl
from jax.experimental.pallas import tpu as pltpu
from jax.sharding import PartitionSpec as P

ADAPTER_SCALE = 2.0
F32 = jnp.float32
BF16 = jnp.bfloat16
CONTRACT_LAST = (((1,), (1,)), ((), ()))
CONTRACT_FIRST = (((0,), (0,)), ((), ()))
VMEM = pl.BlockSpec(memory_space=pltpu.VMEM)
SMEM = pl.BlockSpec(memory_space=pltpu.SMEM)
HBM = pl.BlockSpec(memory_space=pltpu.HBM)
COST = pl.CostEstimate(flops=1, bytes_accessed=1, transcendentals=0)


def params(mib=16):
    return pltpu.CompilerParams(vmem_limit_bytes=mib << 20)


def weight_row(shard, rel, key):
    me = lax.axis_index("fsdp")
    row = jnp.bitwise_xor(me, rel) * shard
    if key is not None:
        row = row + quarter_row(shard, key)
    return row


def quarter_row(shard, key):
    group, data = lax.axis_index("groups"), lax.axis_index("dp")
    a, b = key
    return (((group + a) % 2) * 2 + (data + b) % 2) * (shard // 4)


def dot(a, b, dims=(((1,), (0,)), ((), ()))):
    return lax.dot_general(a, b, dims, preferred_element_type=F32)


def struct(shape, dtype=BF16):
    return jax.ShapeDtypeStruct(shape, dtype)


def prep_kernel(block, cuts, weight, *refs):
    outs, sems = refs[: len(cuts)], refs[len(cuts)]
    copies = []
    for i, (key, start, span) in enumerate(cuts):
        row = pl.multiple_of(quarter_row(weight.shape[0], key), block)
        source = weight.at[pl.ds(row, block), pl.ds(start, span)]
        copies.append(pltpu.make_async_copy(source, outs[i], sems.at[i]))
    for copy in copies:
        copy.start()
    for copy in copies:
        copy.wait()


def load_kernel(count, *refs):
    sems = refs[2 * count]
    copies = [
        pltpu.make_async_copy(refs[i], refs[count + i], sems.at[i]) for i in range(count)
    ]
    for copy in copies:
        copy.start()
    for copy in copies:
        copy.wait()


def low_rank_kernel(slots, rank2, width, kv, place, tok, cot, *refs):
    downs, ups = refs[:slots], refs[slots : 2 * slots]
    spread_low, spread_grad, down_cat, up_cat, keep, send = refs[2 * slots :]
    rows = tok.shape[0]
    me = lax.axis_index("fsdp")
    for r in range(slots):
        down_cat[pl.ds(r * rank2, rank2), :] = downs[r][0]
        up_cat[pl.ds(r * rank2, rank2), :] = ups[r][0]
    pos = me * rows + lax.broadcasted_iota(jnp.int32, (rows, slots * rank2), 0)
    col = lax.broadcasted_iota(jnp.int32, (rows, slots * rank2), 1)
    slot = col // rank2
    is_key = (col % rank2) < (rank2 // 2)
    own = jnp.full((rows, slots * rank2), -1, jnp.int32)
    start = jnp.int32(0)
    for u in range(slots):
        rel = jnp.bitwise_xor(place[slots + u], me)
        own = jnp.where(pos >= start, rel, own)
        start = start + place[u]
    mask = slot == own
    low = jnp.where(mask, dot(tok[...], down_cat[...], CONTRACT_LAST), 0.0).astype(BF16)
    spread_low[...] = low
    back_keys = dot(cot[:, :kv], up_cat[...], CONTRACT_LAST)
    back_vals = dot(cot[:, kv:], up_cat[...], CONTRACT_LAST)
    back = ADAPTER_SCALE * jnp.where(is_key, back_keys, back_vals)
    grad = jnp.where(mask, back, 0.0).astype(BF16)
    spread_grad[...] = grad

    def put(r, cols, value):
        ref = keep if r % 2 == 0 else send
        ref[r // 2, :, cols] = value.astype(BF16)

    step = 1024
    for start in range(0, width, step):
        part = dot(grad, tok[:, start : start + step], CONTRACT_FIRST)
        for r in range(slots):
            put(r, slice(start, start + step), part[r * rank2 : (r + 1) * rank2])
    part_keys = ADAPTER_SCALE * dot(low, cot[:, :kv], CONTRACT_FIRST)
    part_vals = ADAPTER_SCALE * dot(low, cot[:, kv:], CONTRACT_FIRST)
    row = lax.broadcasted_iota(jnp.int32, (slots * rank2, kv), 0)
    part = jnp.where((row % rank2) < (rank2 // 2), part_keys, part_vals)
    for r in range(slots):
        put(r, slice(width, width + kv), part[r * rank2 : (r + 1) * rank2])


def low_rank_call(place, tok, cot, downs, ups):
    slots = len(downs)
    rank2, width = downs[0].shape[1:]
    kv = ups[0].shape[2]
    rows = tok.shape[0]
    half = struct((slots // 2, rank2, width + kv))
    return pl.pallas_call(
        functools.partial(low_rank_kernel, slots, rank2, width, kv),
        out_shape=(
            struct((rows, slots * rank2)),
            struct((rows, slots * rank2)),
            struct((slots * rank2, width)),
            struct((slots * rank2, kv)),
            half,
            half,
        ),
        in_specs=[SMEM] + [VMEM] * (2 + 2 * slots),
        out_specs=(VMEM,) * 6,
        compiler_params=params(),
        cost_estimate=COST,
        name="low_rank",
    )(place, tok, cot, *downs, *ups)


def matmul_kernel(plan, block, shard, rank2, kv, first, last, *refs):
    refs = list(refs)
    tok, cot, low, grad, down, up = (refs.pop(0) for _ in range(6))
    sources = [[refs.pop(0) for _ in range(count)] for count, _, _ in plan]
    if not first:
        acc_in = refs.pop(0)
        refs.pop(0)
    out, gx = refs.pop(0), refs.pop(0)
    stage, sems = refs.pop(0), refs.pop(0)
    acc = out
    if first:
        col = lax.broadcasted_iota(jnp.int32, low.shape, 1)
        is_key = (col % rank2) < (rank2 // 2)
        zero = jnp.zeros(low.shape, BF16)
        low_keys = jnp.where(is_key, low[...], zero)
        low_vals = jnp.where(is_key, zero, low[...])
        acc[:, :kv] = ADAPTER_SCALE * dot(low_keys, up[...])
        acc[:, kv:] = ADAPTER_SCALE * dot(low_vals, up[...])
    copies, pieces = [], []
    for (_, entry, total), chunks in zip(plan, sources):
        for at in range(0, total, block):
            number = len(pieces)
            offset = pl.multiple_of(weight_row(shard, *entry) + at, block)
            where = pl.ds(offset, block)
            back = dot(grad[...], down[:, where])
            start, parts = 0, []
            for chunk in chunks:
                cols = slice(start, start + chunk.shape[1])
                start += chunk.shape[1]
                parts.append((cols, chunk, at))
                back += dot(cot[:, cols], chunk[pl.ds(at, block), :], CONTRACT_LAST)
            stage[number] = back.astype(BF16)
            copy = pltpu.make_async_copy(stage.at[number], gx.at[:, where], sems.at[number])
            copy.start()
            copies.append(copy)
            pieces.append((where, parts))
    edges = sorted({cols.stop for _, parts in pieces for cols, _, _ in parts})
    for low_edge, edge in zip([0] + edges, edges):
        cols = slice(low_edge, edge)
        total = acc[:, cols] if first else acc_in[:, cols]
        for where, parts in pieces:
            span, chunk, at = next(p for p in parts if p[0].stop >= edge)
            inner = slice(low_edge - span.start, edge - span.start)
            total += dot(tok[:, where], chunk[pl.ds(at, block), inner])
        if last:
            out[:, cols] = total.astype(BF16)
        else:
            out[:, cols] = total
    for copy in copies:
        copy.wait()


def matmul_call(shard, tok, cot, low, grad, down, up, sources, prev, last, rank2, name):
    rows, width = tok.shape
    cols = cot.shape[1]
    kv = up.shape[1]
    block = min(512, min(parts[0].shape[0] for _, parts in sources))
    plan = tuple((len(parts), entry, parts[0].shape[0]) for entry, parts in sources)
    flops = 4 * rows * cols * sum(total for _, _, total in plan)
    cost = pl.CostEstimate(flops=flops, bytes_accessed=1, transcendentals=0)
    count = sum(total // block for _, _, total in plan)
    arrays = [part for _, parts in sources for part in parts]
    args = [tok, cot, low, grad, down, up] + arrays
    in_specs = [VMEM] * (6 + len(arrays))
    first = prev is None
    aliases = {}
    if not first:
        args += list(prev)
        in_specs += [VMEM, HBM]
        aliases = {len(args) - 1: 1}
        if not last:
            aliases[len(args) - 2] = 0
    scratch = [pltpu.VMEM((count, rows, block), BF16), pltpu.SemaphoreType.DMA((count,))]
    return pl.pallas_call(
        functools.partial(matmul_kernel, plan, block, shard, rank2, kv, first, last),
        out_shape=(struct((rows, cols), BF16 if last else F32), struct((rows, width))),
        in_specs=in_specs,
        out_specs=(VMEM, HBM),
        scratch_shapes=scratch,
        input_output_aliases=aliases,
        compiler_params=params(),
        cost_estimate=cost,
        name=name,
    )(*args)


def even_odd_kernel(keep, recv, even, odd):
    for i in range(even.shape[0]):
        for out, j in ((even, 2 * i), (odd, 2 * i + 1)):
            out[i] = (keep[j].astype(F32) + recv[j].astype(F32)).astype(BF16)


def halves_kernel(keep, recv, mine, other):
    half = mine.shape[0]
    parity = lax.axis_index("dp") % 2
    for out, upper in ((mine, parity), (other, 1 - parity)):
        row = pl.ds(pl.multiple_of(upper * half, half), half)
        out[...] = (keep[0, row, :].astype(F32) + recv[0, row, :].astype(F32)).astype(BF16)


def finish_kernel(width, mine, recv, down, up):
    half = mine.shape[0]
    parity = lax.axis_index("dp") % 2
    for part, upper in ((mine, parity), (recv, 1 - parity)):
        row = pl.ds(pl.multiple_of(upper * half, half), half)
        down[0, row, :] = part[:, :width].astype(F32)
        up[0, row, :] = part[:, width:].astype(F32)


def xor_swap(value, axis, size, bit):
    return lax.ppermute(value, axis, [(i, i ^ bit) for i in range(size)])


PREP_MIB = 54
SPANS = (4, 8, 4)


def per_device(
    n_groups,
    n_dp,
    n_fsdp,
    tokens,
    key_value_weight,
    adapter_down_maps,
    adapter_up_maps,
    counts,
    tenant_slot_index,
    cotangent,
):
    rows, width = tokens.shape
    slots = tenant_slot_index.shape[0]
    rank2 = adapter_down_maps.shape[1]
    kv = adapter_up_maps.shape[2]
    shard = key_value_weight.shape[0]
    cols = key_value_weight.shape[1]
    swap = lambda value, bit: xor_swap(value, "fsdp", n_fsdp, bit)
    swap_y = lambda value: xor_swap(value, "groups", n_groups, 1)
    swap_z = lambda value: xor_swap(value, "dp", n_dp, 1)
    high_bits = [b for b in range(2, n_fsdp, 2)]
    quartered = n_groups == 2 and n_dp % 2 == 0 and n_fsdp == 4 and shard % 1024 == 0
    block = shard // 4
    place = jnp.concatenate([counts[0], tenant_slot_index])

    def local(kernel, outs, args, name, scratch=(), spaces=None, mib=16):
        spaces = spaces or [SMEM if a is place else VMEM for a in args]
        return pl.pallas_call(
            kernel,
            out_shape=tuple(outs),
            in_specs=spaces,
            out_specs=(VMEM,) * len(outs),
            scratch_shapes=list(scratch),
            compiler_params=params(mib),
            cost_estimate=COST,
            name=name,
        )(*args)

    barrier = lambda *values: lax.optimization_barrier(values)

    downs, ups = {0: adapter_down_maps}, {0: adapter_up_maps}
    for bit in high_bits + [1]:
        downs[bit], ups[bit] = swap(adapter_down_maps, bit), swap(adapter_up_maps, bit)
    sibling = swap(key_value_weight, 1)

    span = cols // 4
    if quartered:
        cuts, start = [], 0
        for size in SPANS:
            cuts.append(((0, 0), start * cols // 16, size * cols // 16))
            start += size
        start = SPANS[0] * cols // 16
        cuts.append(((1, 1), start, cols - start))
        sent = local(
            functools.partial(prep_kernel, block, cuts[:1]),
            [struct((block, size)) for _, _, size in cuts[:1]],
            (key_value_weight,),
            "prep",
            [pltpu.SemaphoreType.DMA((1,))],
            [HBM],
            PREP_MIB,
        )
        direct = [swap(sent[0], 2)]
        sent = list(sent) + list(
            local(
                functools.partial(prep_kernel, block, cuts[1:]),
                [struct((block, size)) for _, _, size in cuts[1:]],
                (key_value_weight,),
                "split",
                [pltpu.SemaphoreType.DMA((len(cuts) - 1,))],
                [HBM],
            )
        )
        first, second, *rest = sent
    loads = (tokens, cotangent, key_value_weight)
    tok, cot, weight = local(
        functools.partial(load_kernel, len(loads)),
        [struct(a.shape) for a in loads],
        loads,
        "load",
        [pltpu.SemaphoreType.DMA((len(loads),))],
        [HBM] * len(loads),
    )
    if quartered:
        direct[0], downs[2], ups[2], tok, second, sibling, *rest = barrier(
            direct[0], downs[2], ups[2], tok, second, sibling, *rest
        )
    for bit in high_bits:
        downs[bit], ups[bit], tok = barrier(downs[bit], ups[bit], tok)
        downs[bit + 1], ups[bit + 1] = swap(downs[bit], 1), swap(ups[bit], 1)

    low, grad, down_cat, up_cat, keep, send = low_rank_call(
        place, tok, cot, [downs[r] for r in range(slots)], [ups[r] for r in range(slots)]
    )

    def matmul(number, sources, prev, last=False):
        return matmul_call(
            shard,
            tok,
            cot,
            low,
            grad,
            down_cat,
            up_cat,
            sources,
            prev,
            last,
            rank2,
            f"matmul_{number}",
        )

    add = lambda a, b: (a.astype(F32) + b.astype(F32)).astype(BF16)
    half = struct((rank2 // 2, width + kv))
    finish = lambda mine, recv: local(
        functools.partial(finish_kernel, width),
        (struct((1, rank2, width), F32), struct((1, rank2, kv), F32)),
        (mine, recv),
        "finish",
    )
    recv = swap(send, 1)
    if not quartered:
        bit = 2
        while bit < n_fsdp:
            parts = struct((keep.shape[0] // 2,) + keep.shape[1:])
            keep, send = local(even_odd_kernel, (parts, parts), (keep, recv), "even_odd")
            recv = swap(send, bit)
            bit *= 2
        if n_dp == 1:
            total = add(keep[0], recv[0]).astype(F32)
            grad_down, grad_up = total[None, :, :width], total[None, :, width:]
        else:
            mine, other = local(halves_kernel, (half, half), (keep, recv), "halves")
            mine = add(mine, swap_z(other))
            bit = 2
            while bit < n_dp:
                mine = add(mine, xor_swap(mine, "dp", n_dp, bit))
                bit *= 2
            grad_down, grad_up = finish(mine, swap_z(mine))
        calls = [
            [((0, None), [weight])],
            [((1, None), [sibling])],
        ]
        for bit in high_bits:
            through = swap(key_value_weight, bit)
            calls.append(
                [
                    ((bit, None), [through]),
                    ((bit + 1, None), [swap(through, 1)]),
                ]
            )
        prev = None
        for number, sources in enumerate(calls):
            prev = matmul(number, sources, prev, number == len(calls) - 1)
        return prev[0], prev[1], grad_down, grad_up

    link = [keep]

    def after(*values):
        held = barrier(*values, *link)[: len(values)]
        link[:] = held[:1]
        return held if len(values) > 1 else held[0]

    def ready(values):
        held = after(*values)
        return list(held) if len(values) > 1 else [held]

    core = lambda parts: [swap(c, 1) for c in parts]
    parts = struct((1,) + keep.shape[1:])
    via_y, via_z = [swap_y(direct[0])], [swap_z(direct[0])]
    keep, recv = after(keep, recv)
    keep, send = local(even_odd_kernel, (parts, parts), (keep, recv), "even_odd")
    keep, send = after(keep, send)
    recv = swap(send, 2)
    low = after(low)
    prev = matmul(0, [((0, None), [weight])], None)
    second, *rest = after(second, *rest, *prev)[: len(sent) - 1]
    direct += [swap(c, 2) for c in (second, rest[0])]
    across = swap(rest[1], 2)
    recv, keep = after(recv, keep)
    mine, other = local(halves_kernel, (half, half), (keep, recv), "halves")
    mine, other = after(mine, other)
    recv = swap_z(other)
    via_z[0], via_y[0] = after(via_z[0], via_y[0])
    diagonal = [swap_y(via_z[0])]
    prev = after(*prev)
    prev = matmul(1, [((1, None), [sibling])], prev)
    prev = after(*prev)
    mine, recv = after(mine, recv)
    mine = after(add(mine, recv))
    bit = 2
    recv = xor_swap(mine, "dp", n_dp, bit) if n_dp > 2 else None
    diagonal[0] = after(diagonal[0])
    direct[1] = after(direct[1])
    via_y.append(swap_y(direct[1]))
    via_z.append(swap_z(direct[1]))
    direct[2] = after(direct[2])
    via_y.append(swap_y(direct[2]))
    via_z.append(swap_z(direct[2]))
    while bit < n_dp:
        if bit > 2:
            recv = xor_swap(mine, "dp", n_dp, bit)
        mine, recv = after(mine, recv)
        mine = after(add(mine, recv))
        bit *= 2
    other = swap_z(mine)

    prev = matmul(2, [((2, (0, 0)), direct)], prev)
    prev = after(*prev)
    mine, other = after(mine, other)
    grad_down, grad_up = after(*finish(mine, other))
    via_y[1], via_z[1] = after(via_y[1], via_z[1])
    via_y[2], via_z[2] = after(via_y[2], via_z[2])
    prev = matmul(3, [((2, (1, 0)), via_y), ((2, (0, 1)), via_z)], prev)
    prev = after(*prev)
    diagonal.append(after(across))
    crossed = [core(p) for p in (direct, diagonal, via_y, via_z)]
    prev = matmul(4, [((2, (1, 1)), diagonal)], prev)
    keys = ((0, 0), (1, 1), (1, 0), (0, 1))
    sources = [((3, key), p) for key, p in zip(keys, crossed)]
    prev = matmul(5, sources, prev, True)
    return prev[0], prev[1], grad_down, grad_up


def solution(mesh):
    in_specs = (
        P(("groups", "dp", "fsdp"), None),
        P("fsdp", None),
        P(("groups", "fsdp"), None, None),
        P(("groups", "fsdp"), None, None),
        P(("groups", "dp"), None),
        P("groups"),
        P(("groups", "dp", "fsdp"), None),
    )
    out_specs = (
        P(("groups", "dp", "fsdp"), None),
        P(("groups", "dp", "fsdp"), None),
        P(("groups", "fsdp"), None, None),
        P(("groups", "fsdp"), None, None),
    )
    body = functools.partial(
        per_device, mesh.shape["groups"], mesh.shape["dp"], mesh.shape["fsdp"]
    )
    return jax.shard_map(
        body, mesh=mesh, in_specs=in_specs, out_specs=out_specs, check_vma=False
    )
```

```python
import functools

import jax
import jax.numpy as jnp
from jax import lax
from jax.experimental import pallas as pl
from jax.experimental.pallas import tpu as pltpu
from jax.sharding import PartitionSpec as P

ADAPTER_SCALE = 2.0
F32 = jnp.float32
BF16 = jnp.bfloat16
CONTRACT_LAST = (((1,), (1,)), ((), ()))
CONTRACT_FIRST = (((0,), (0,)), ((), ()))
VMEM = pl.BlockSpec(memory_space=pltpu.VMEM)
SMEM = pl.BlockSpec(memory_space=pltpu.SMEM)
HBM = pl.BlockSpec(memory_space=pltpu.HBM)
COST = pl.CostEstimate(flops=1, bytes_accessed=1, transcendentals=0)


def params(mib=16):
    return pltpu.CompilerParams(vmem_limit_bytes=mib << 20)


def weight_row(shard, rel, key):
    me = lax.axis_index("fsdp")
    row = jnp.bitwise_xor(me, rel) * shard
    if key is not None:
        row = row + quarter_row(shard, key)
    return row


def quarter_row(shard, key):
    group, data = lax.axis_index("groups"), lax.axis_index("dp")
    a, b = key
    return (((group + a) % 2) * 2 + (data + b) % 2) * (shard // 4)


def dot(a, b, dims=(((1,), (0,)), ((), ()))):
    return lax.dot_general(a, b, dims, preferred_element_type=F32)


def struct(shape, dtype=BF16):
    return jax.ShapeDtypeStruct(shape, dtype)


def prep_kernel(block, cuts, weight, *refs):
    outs, sems = refs[: len(cuts)], refs[len(cuts)]
    copies = []
    for i, (key, start, span) in enumerate(cuts):
        row = pl.multiple_of(quarter_row(weight.shape[0], key), block)
        source = weight.at[pl.ds(row, block), pl.ds(start, span)]
        copies.append(pltpu.make_async_copy(source, outs[i], sems.at[i]))
    for copy in copies:
        copy.start()
    for copy in copies:
        copy.wait()


def pack_kernel(block, cuts, weight, down, up, pack, *refs):
    outs, sems = refs[: len(cuts)], refs[len(cuts)]
    width = down.shape[2]
    moves = [
        (down.at[0], pack.at[:, pl.ds(0, width)]),
        (up.at[0], pack.at[:, pl.ds(width, up.shape[2])]),
    ]
    for out, (key, start, span) in zip(outs, cuts):
        row = pl.multiple_of(quarter_row(weight.shape[0], key), block)
        moves.append((weight.at[pl.ds(row, block), pl.ds(start, span)], out))
    copies = [pltpu.make_async_copy(a, b, sems.at[i]) for i, (a, b) in enumerate(moves)]
    for copy in copies:
        copy.start()
    for copy in copies:
        copy.wait()


def load_kernel(count, *refs):
    sems = refs[2 * count]
    copies = [
        pltpu.make_async_copy(refs[i], refs[count + i], sems.at[i]) for i in range(count)
    ]
    for copy in copies:
        copy.start()
    for copy in copies:
        copy.wait()


def low_rank_kernel(slots, rank2, width, kv, place, tok, cot, *refs):
    packs = refs[:slots]
    spread_low, spread_grad, down_cat, up_cat, keep, send = refs[slots:]
    rows = tok.shape[0]
    me = lax.axis_index("fsdp")
    for r in range(slots):
        down_cat[pl.ds(r * rank2, rank2), :] = packs[r][:, :width]
        up_cat[pl.ds(r * rank2, rank2), :] = packs[r][:, width:]
    pos = me * rows + lax.broadcasted_iota(jnp.int32, (rows, slots * rank2), 0)
    col = lax.broadcasted_iota(jnp.int32, (rows, slots * rank2), 1)
    slot = col // rank2
    is_key = (col % rank2) < (rank2 // 2)
    own = jnp.full((rows, slots * rank2), -1, jnp.int32)
    start = jnp.int32(0)
    for u in range(slots):
        rel = jnp.bitwise_xor(place[slots + u], me)
        own = jnp.where(pos >= start, rel, own)
        start = start + place[u]
    mask = slot == own
    low = jnp.where(mask, dot(tok[...], down_cat[...], CONTRACT_LAST), 0.0).astype(BF16)
    spread_low[...] = low
    back_keys = dot(cot[:, :kv], up_cat[...], CONTRACT_LAST)
    back_vals = dot(cot[:, kv:], up_cat[...], CONTRACT_LAST)
    back = ADAPTER_SCALE * jnp.where(is_key, back_keys, back_vals)
    grad = jnp.where(mask, back, 0.0).astype(BF16)
    spread_grad[...] = grad

    def put(r, cols, value):
        ref = keep if r % 2 == 0 else send
        ref[r // 2, :, cols] = value.astype(BF16)

    step = 1024
    for start in range(0, width, step):
        part = dot(grad, tok[:, start : start + step], CONTRACT_FIRST)
        for r in range(slots):
            put(r, slice(start, start + step), part[r * rank2 : (r + 1) * rank2])
    part_keys = ADAPTER_SCALE * dot(low, cot[:, :kv], CONTRACT_FIRST)
    part_vals = ADAPTER_SCALE * dot(low, cot[:, kv:], CONTRACT_FIRST)
    row = lax.broadcasted_iota(jnp.int32, (slots * rank2, kv), 0)
    part = jnp.where((row % rank2) < (rank2 // 2), part_keys, part_vals)
    for r in range(slots):
        put(r, slice(width, width + kv), part[r * rank2 : (r + 1) * rank2])


def low_rank_call(place, tok, cot, packs, width, kv):
    slots = len(packs)
    rank2 = packs[0].shape[0]
    rows = tok.shape[0]
    half = struct((slots // 2, rank2, width + kv))
    return pl.pallas_call(
        functools.partial(low_rank_kernel, slots, rank2, width, kv),
        out_shape=(
            struct((rows, slots * rank2)),
            struct((rows, slots * rank2)),
            struct((slots * rank2, width)),
            struct((slots * rank2, kv)),
            half,
            half,
        ),
        in_specs=[SMEM] + [VMEM] * (2 + slots),
        out_specs=(VMEM,) * 6,
        compiler_params=params(),
        cost_estimate=COST,
        name="low_rank",
    )(place, tok, cot, *packs)


def matmul_kernel(plan, block, shard, rank2, kv, first, last, *refs):
    refs = list(refs)
    tok, cot, low, grad, down, up = (refs.pop(0) for _ in range(6))
    sources = [[refs.pop(0) for _ in range(count)] for count, _, _ in plan]
    if not first:
        acc_in = refs.pop(0)
        refs.pop(0)
    out, gx = refs.pop(0), refs.pop(0)
    stage, sems = refs.pop(0), refs.pop(0)
    acc = out
    if first:
        col = lax.broadcasted_iota(jnp.int32, low.shape, 1)
        is_key = (col % rank2) < (rank2 // 2)
        zero = jnp.zeros(low.shape, BF16)
        low_keys = jnp.where(is_key, low[...], zero)
        low_vals = jnp.where(is_key, zero, low[...])
        acc[:, :kv] = ADAPTER_SCALE * dot(low_keys, up[...])
        acc[:, kv:] = ADAPTER_SCALE * dot(low_vals, up[...])
    copies, pieces = [], []
    for (_, entry, total), chunks in zip(plan, sources):
        for at in range(0, total, block):
            number = len(pieces)
            offset = pl.multiple_of(weight_row(shard, *entry) + at, block)
            where = pl.ds(offset, block)
            back = dot(grad[...], down[:, where])
            start, parts = 0, []
            for chunk in chunks:
                cols = slice(start, start + chunk.shape[1])
                start += chunk.shape[1]
                parts.append((cols, chunk, at))
                back += dot(cot[:, cols], chunk[pl.ds(at, block), :], CONTRACT_LAST)
            stage[number] = back.astype(BF16)
            copy = pltpu.make_async_copy(stage.at[number], gx.at[:, where], sems.at[number])
            copy.start()
            copies.append(copy)
            pieces.append((where, parts))
    edges = sorted({cols.stop for _, parts in pieces for cols, _, _ in parts})
    for low_edge, edge in zip([0] + edges, edges):
        cols = slice(low_edge, edge)
        total = acc[:, cols] if first else acc_in[:, cols]
        for where, parts in pieces:
            span, chunk, at = next(p for p in parts if p[0].stop >= edge)
            inner = slice(low_edge - span.start, edge - span.start)
            total += dot(tok[:, where], chunk[pl.ds(at, block), inner])
        if last:
            out[:, cols] = total.astype(BF16)
        else:
            out[:, cols] = total
    for copy in copies:
        copy.wait()


def matmul_call(shard, tok, cot, low, grad, down, up, sources, prev, last, rank2, name):
    rows, width = tok.shape
    cols = cot.shape[1]
    kv = up.shape[1]
    block = min(512, min(parts[0].shape[0] for _, parts in sources))
    plan = tuple((len(parts), entry, parts[0].shape[0]) for entry, parts in sources)
    flops = 4 * rows * cols * sum(total for _, _, total in plan)
    cost = pl.CostEstimate(flops=flops, bytes_accessed=1, transcendentals=0)
    count = sum(total // block for _, _, total in plan)
    arrays = [part for _, parts in sources for part in parts]
    args = [tok, cot, low, grad, down, up] + arrays
    in_specs = [VMEM] * (6 + len(arrays))
    first = prev is None
    aliases = {}
    if not first:
        args += list(prev)
        in_specs += [VMEM, HBM]
        aliases = {len(args) - 1: 1}
        if not last:
            aliases[len(args) - 2] = 0
    scratch = [pltpu.VMEM((count, rows, block), BF16), pltpu.SemaphoreType.DMA((count,))]
    return pl.pallas_call(
        functools.partial(matmul_kernel, plan, block, shard, rank2, kv, first, last),
        out_shape=(struct((rows, cols), BF16 if last else F32), struct((rows, width))),
        in_specs=in_specs,
        out_specs=(VMEM, HBM),
        scratch_shapes=scratch,
        input_output_aliases=aliases,
        compiler_params=params(),
        cost_estimate=cost,
        name=name,
    )(*args)


def even_odd_kernel(keep, recv, even, odd):
    for i in range(even.shape[0]):
        for out, j in ((even, 2 * i), (odd, 2 * i + 1)):
            out[i] = (keep[j].astype(F32) + recv[j].astype(F32)).astype(BF16)


def halves_kernel(keep, recv, mine, other):
    half = mine.shape[0]
    parity = lax.axis_index("dp") % 2
    for out, upper in ((mine, parity), (other, 1 - parity)):
        row = pl.ds(pl.multiple_of(upper * half, half), half)
        out[...] = (keep[0, row, :].astype(F32) + recv[0, row, :].astype(F32)).astype(BF16)


def finish_kernel(width, mine, recv, down, up):
    half = mine.shape[0]
    parity = lax.axis_index("dp") % 2
    for part, upper in ((mine, parity), (recv, 1 - parity)):
        row = pl.ds(pl.multiple_of(upper * half, half), half)
        down[0, row, :] = part[:, :width].astype(F32)
        up[0, row, :] = part[:, width:].astype(F32)


def xor_swap(value, axis, size, bit):
    return lax.ppermute(value, axis, [(i, i ^ bit) for i in range(size)])


PREP_MIB = 54
SPANS = (7, 9)
DIAGONAL_AT = 1
CORE_AT = 1
CORE_GATE = False
DIAGONAL_MM = True
LATE_FINISH = True


def per_device(
    n_groups,
    n_dp,
    n_fsdp,
    tokens,
    key_value_weight,
    adapter_down_maps,
    adapter_up_maps,
    counts,
    tenant_slot_index,
    cotangent,
):
    rows, width = tokens.shape
    slots = tenant_slot_index.shape[0]
    rank2 = adapter_down_maps.shape[1]
    kv = adapter_up_maps.shape[2]
    shard = key_value_weight.shape[0]
    cols = key_value_weight.shape[1]
    swap = lambda value, bit: xor_swap(value, "fsdp", n_fsdp, bit)
    swap_y = lambda value: xor_swap(value, "groups", n_groups, 1)
    swap_z = lambda value: xor_swap(value, "dp", n_dp, 1)
    high_bits = [b for b in range(2, n_fsdp, 2)]
    quartered = n_groups == 2 and n_dp % 2 == 0 and n_fsdp == 4 and shard % 1024 == 0
    block = shard // 4
    place = jnp.concatenate([counts[0], tenant_slot_index])

    def local(kernel, outs, args, name, scratch=(), spaces=None, mib=16):
        spaces = spaces or [SMEM if a is place else VMEM for a in args]
        return pl.pallas_call(
            kernel,
            out_shape=tuple(outs),
            in_specs=spaces,
            out_specs=(VMEM,) * len(outs),
            scratch_shapes=list(scratch),
            compiler_params=params(mib),
            cost_estimate=COST,
            name=name,
        )(*args)

    barrier = lambda *values: lax.optimization_barrier(values)

    cuts, start = [], 0
    if quartered:
        for size in SPANS:
            cuts.append(((0, 0), start * cols // 16, size * cols // 16))
            start += size
        start = SPANS[0] * cols // 16
        cuts.append(((1, 1), start, cols - start))

    pack, *sent = local(
        functools.partial(pack_kernel, block, cuts[:1]),
        [struct((rank2, width + kv))] + [struct((block, size)) for _, _, size in cuts[:1]],
        (key_value_weight, adapter_down_maps, adapter_up_maps),
        "prep",
        [pltpu.SemaphoreType.DMA((2 + len(cuts[:1]),))],
        [HBM, HBM, HBM],
        PREP_MIB,
    )
    packs = {0: pack}
    for bit in high_bits + [1]:
        packs[bit] = swap(pack, bit)
    sibling = swap(key_value_weight, 1)
    if quartered:
        direct = [swap(sent[0], 2)]
        sent = list(sent) + list(
            local(
                functools.partial(prep_kernel, block, cuts[1:]),
                [struct((block, size)) for _, _, size in cuts[1:]],
                (key_value_weight,),
                "split",
                [pltpu.SemaphoreType.DMA((len(cuts) - 1,))],
                [HBM],
            )
        )
        first, second, *rest = sent
    loads = (tokens, cotangent, key_value_weight)
    tok, cot, weight = local(
        functools.partial(load_kernel, len(loads)),
        [struct(a.shape) for a in loads],
        loads,
        "load",
        [pltpu.SemaphoreType.DMA((len(loads),))],
        [HBM] * len(loads),
    )
    if quartered:
        packs[2], tok, second, sibling, *rest = barrier(
            packs[2], tok, second, sibling, *rest
        )
    for bit in high_bits:
        packs[bit], tok = barrier(packs[bit], tok)
        packs[bit + 1] = swap(packs[bit], 1)

    if quartered:
        direct[0], tok, packs[3] = barrier(direct[0], tok, packs[3])
    low, grad, down_cat, up_cat, keep, send = low_rank_call(
        place, tok, cot, [packs[r] for r in range(slots)], width, kv
    )

    def matmul(number, sources, prev, last=False):
        return matmul_call(
            shard,
            tok,
            cot,
            low,
            grad,
            down_cat,
            up_cat,
            sources,
            prev,
            last,
            rank2,
            f"matmul_{number}",
        )

    add = lambda a, b: (a.astype(F32) + b.astype(F32)).astype(BF16)
    half = struct((rank2 // 2, width + kv))
    finish = lambda mine, recv: local(
        functools.partial(finish_kernel, width),
        (struct((1, rank2, width), F32), struct((1, rank2, kv), F32)),
        (mine, recv),
        "finish",
    )
    recv = swap(send, 1)
    if not quartered:
        bit = 2
        while bit < n_fsdp:
            parts = struct((keep.shape[0] // 2,) + keep.shape[1:])
            keep, send = local(even_odd_kernel, (parts, parts), (keep, recv), "even_odd")
            recv = swap(send, bit)
            bit *= 2
        if n_dp == 1:
            total = add(keep[0], recv[0]).astype(F32)
            grad_down, grad_up = total[None, :, :width], total[None, :, width:]
        else:
            mine, other = local(halves_kernel, (half, half), (keep, recv), "halves")
            mine = add(mine, swap_z(other))
            bit = 2
            while bit < n_dp:
                mine = add(mine, xor_swap(mine, "dp", n_dp, bit))
                bit *= 2
            grad_down, grad_up = finish(mine, swap_z(mine))
        calls = [
            [((0, None), [weight])],
            [((1, None), [sibling])],
        ]
        for bit in high_bits:
            through = swap(key_value_weight, bit)
            calls.append(
                [
                    ((bit, None), [through]),
                    ((bit + 1, None), [swap(through, 1)]),
                ]
            )
        prev = None
        for number, sources in enumerate(calls):
            prev = matmul(number, sources, prev, number == len(calls) - 1)
        return prev[0], prev[1], grad_down, grad_up

    link = [keep]

    def after(*values):
        held = barrier(*values, *link)[: len(values)]
        link[:] = held[:1]
        return held if len(values) > 1 else held[0]

    def ready(values):
        held = after(*values)
        return list(held) if len(values) > 1 else [held]

    core = lambda parts: [swap(c, 1) for c in parts]
    parts = struct((1,) + keep.shape[1:])
    ahead = core(direct)
    via_y, via_z = [swap_y(direct[0])], [swap_z(direct[0])]
    keep, recv, ahead[0] = after(keep, recv, ahead[0])
    keep, send = local(even_odd_kernel, (parts, parts), (keep, recv), "even_odd")
    keep, send = after(keep, send)
    recv = swap(send, 2)
    low = after(low)
    prev = matmul(0, [((0, None), [weight])], None)
    rest = list(after(*sent[1:], *prev)[: len(sent) - 1])
    direct += [swap(c, 2) for c in rest[:-1]]
    across = swap(rest[-1], 2)
    recv, keep = after(recv, keep)
    mine, other = local(halves_kernel, (half, half), (keep, recv), "halves")
    mine, other = after(mine, other)
    recv = swap_z(other)
    via_z[0], via_y[0] = after(via_z[0], via_y[0])
    diagonal = [swap_y(via_z[0])]
    prev = after(*prev)
    prev = matmul(1, [((1, None), [sibling])], prev)
    prev = after(*prev)
    mine, recv = after(mine, recv)
    mine = after(add(mine, recv))
    bit = 2
    recv = xor_swap(mine, "dp", n_dp, bit) if n_dp > 2 else None
    for i in range(1, len(direct)):
        direct[i] = after(direct[i])
        via_y.append(swap_y(direct[i]))
        via_z.append(swap_z(direct[i]))
        if i == 1 and DIAGONAL_AT == 1:
            diagonal[0] = after(diagonal[0])
    while bit < n_dp:
        if bit > 2:
            recv = xor_swap(mine, "dp", n_dp, bit)
        mine, recv = after(mine, recv)
        mine = after(add(mine, recv))
        bit *= 2
    other = swap_z(mine)
    if DIAGONAL_AT == 2:
        diagonal[0] = after(diagonal[0])

    if CORE_AT == 1:
        ahead[1:] = ready(ahead[:1] + core(direct[1:]))[1:]
    sources = [((2, (0, 0)), direct)]
    if CORE_AT == 1:
        sources.append(((3, (0, 0)), ahead))
    prev = matmul(2, sources, prev)
    prev = after(*prev)
    if not LATE_FINISH:
        mine, other = after(mine, other)
        grad_down, grad_up = after(*finish(mine, other))
    if DIAGONAL_AT == 3:
        diagonal[0] = after(diagonal[0])
    diagonal.append(after(across))
    if DIAGONAL_MM:
        prev = matmul(3, [((2, (1, 1)), diagonal)], prev)
        prev = after(*prev)
    for i in range(1, len(direct)):
        via_y[i], via_z[i] = after(via_y[i], via_z[i])
    groups = [diagonal, via_y, via_z]
    if CORE_AT != 1:
        groups.append(direct)
    if CORE_GATE:
        flat = iter(after(*[p for group in groups for p in group]))
        groups = [[next(flat) for _ in group] for group in groups]
    crossed = [core(p) for p in groups[:3]]
    if CORE_AT != 1:
        crossed.append(ahead + core(groups[3][1:]))
    sources = [((2, (1, 0)), via_y), ((2, (0, 1)), via_z)]
    if not DIAGONAL_MM:
        sources.append(((2, (1, 1)), diagonal))
    prev = matmul(4, sources, prev)
    if LATE_FINISH:
        prev = after(*prev)
        mine, other = after(mine, other)
        grad_down, grad_up = after(*finish(mine, other))
    keys = ((1, 1), (1, 0), (0, 1), (0, 0))
    sources = [((3, key), p) for key, p in zip(keys, crossed)]
    prev = matmul(5, sources, prev, True)
    return prev[0], prev[1], grad_down, grad_up


def solution(mesh):
    in_specs = (
        P(("groups", "dp", "fsdp"), None),
        P("fsdp", None),
        P(("groups", "fsdp"), None, None),
        P(("groups", "fsdp"), None, None),
        P(("groups", "dp"), None),
        P("groups"),
        P(("groups", "dp", "fsdp"), None),
    )
    out_specs = (
        P(("groups", "dp", "fsdp"), None),
        P(("groups", "dp", "fsdp"), None),
        P(("groups", "fsdp"), None, None),
        P(("groups", "fsdp"), None, None),
    )
    body = functools.partial(
        per_device, mesh.shape["groups"], mesh.shape["dp"], mesh.shape["fsdp"]
    )
    return jax.shard_map(
        body, mesh=mesh, in_specs=in_specs, out_specs=out_specs, check_vma=False
    )
```

```python
import functools

import jax
import jax.numpy as jnp
from jax import lax
from jax.experimental import pallas as pl
from jax.experimental.pallas import tpu as pltpu
from jax.sharding import PartitionSpec as P

ADAPTER_SCALE = 2.0
F32 = jnp.float32
BF16 = jnp.bfloat16
CONTRACT_LAST = (((1,), (1,)), ((), ()))
CONTRACT_FIRST = (((0,), (0,)), ((), ()))
VMEM = pl.BlockSpec(memory_space=pltpu.VMEM)
SMEM = pl.BlockSpec(memory_space=pltpu.SMEM)
HBM = pl.BlockSpec(memory_space=pltpu.HBM)
COST = pl.CostEstimate(flops=1, bytes_accessed=1, transcendentals=0)


def params(mib=16):
    return pltpu.CompilerParams(vmem_limit_bytes=mib << 20)


def weight_row(shard, rel, key):
    me = lax.axis_index("fsdp")
    row = jnp.bitwise_xor(me, rel) * shard
    if key is not None:
        row = row + quarter_row(shard, key)
    return row


def quarter_row(shard, key):
    group, data = lax.axis_index("groups"), lax.axis_index("dp")
    a, b = key
    return (((group + a) % 2) * 2 + (data + b) % 2) * (shard // 4)


def dot(a, b, dims=(((1,), (0,)), ((), ()))):
    return lax.dot_general(a, b, dims, preferred_element_type=F32)


def struct(shape, dtype=BF16):
    return jax.ShapeDtypeStruct(shape, dtype)


def prep_kernel(block, cuts, weight, *refs):
    outs, sems = refs[: len(cuts)], refs[len(cuts)]
    copies = []
    for i, (key, start, span) in enumerate(cuts):
        row = pl.multiple_of(quarter_row(weight.shape[0], key), block)
        source = weight.at[pl.ds(row, block), pl.ds(start, span)]
        copies.append(pltpu.make_async_copy(source, outs[i], sems.at[i]))
    for copy in copies:
        copy.start()
    for copy in copies:
        copy.wait()


def pack_kernel(block, cuts, weight, down, up, pack, *refs):
    outs, sems = refs[: len(cuts)], refs[len(cuts)]
    width = down.shape[2]
    moves = [
        (down.at[0], pack.at[:, pl.ds(0, width)]),
        (up.at[0], pack.at[:, pl.ds(width, up.shape[2])]),
    ]
    for out, (key, start, span) in zip(outs, cuts):
        row = pl.multiple_of(quarter_row(weight.shape[0], key), block)
        moves.append((weight.at[pl.ds(row, block), pl.ds(start, span)], out))
    copies = [pltpu.make_async_copy(a, b, sems.at[i]) for i, (a, b) in enumerate(moves)]
    for copy in copies:
        copy.start()
    for copy in copies:
        copy.wait()


def load_kernel(count, *refs):
    sems = refs[2 * count]
    copies = [
        pltpu.make_async_copy(refs[i], refs[count + i], sems.at[i]) for i in range(count)
    ]
    for copy in copies:
        copy.start()
    for copy in copies:
        copy.wait()


def low_rank_kernel(slots, rank2, width, kv, place, tok, cot, *refs):
    packs = refs[:slots]
    spread_low, spread_grad, down_cat, up_cat, keep, send = refs[slots:]
    rows = tok.shape[0]
    me = lax.axis_index("fsdp")
    for r in range(slots):
        down_cat[pl.ds(r * rank2, rank2), :] = packs[r][:, :width]
        up_cat[pl.ds(r * rank2, rank2), :] = packs[r][:, width:]
    pos = me * rows + lax.broadcasted_iota(jnp.int32, (rows, slots * rank2), 0)
    col = lax.broadcasted_iota(jnp.int32, (rows, slots * rank2), 1)
    slot = col // rank2
    is_key = (col % rank2) < (rank2 // 2)
    own = jnp.full((rows, slots * rank2), -1, jnp.int32)
    start = jnp.int32(0)
    for u in range(slots):
        rel = jnp.bitwise_xor(place[slots + u], me)
        own = jnp.where(pos >= start, rel, own)
        start = start + place[u]
    mask = slot == own
    low = jnp.where(mask, dot(tok[...], down_cat[...], CONTRACT_LAST), 0.0).astype(BF16)
    spread_low[...] = low
    back_keys = dot(cot[:, :kv], up_cat[...], CONTRACT_LAST)
    back_vals = dot(cot[:, kv:], up_cat[...], CONTRACT_LAST)
    back = ADAPTER_SCALE * jnp.where(is_key, back_keys, back_vals)
    grad = jnp.where(mask, back, 0.0).astype(BF16)
    spread_grad[...] = grad

    def put(r, cols, value):
        ref = keep if r % 2 == 0 else send
        ref[r // 2, :, cols] = value.astype(BF16)

    step = 1024
    for start in range(0, width, step):
        part = dot(grad, tok[:, start : start + step], CONTRACT_FIRST)
        for r in range(slots):
            put(r, slice(start, start + step), part[r * rank2 : (r + 1) * rank2])
    part_keys = ADAPTER_SCALE * dot(low, cot[:, :kv], CONTRACT_FIRST)
    part_vals = ADAPTER_SCALE * dot(low, cot[:, kv:], CONTRACT_FIRST)
    row = lax.broadcasted_iota(jnp.int32, (slots * rank2, kv), 0)
    part = jnp.where((row % rank2) < (rank2 // 2), part_keys, part_vals)
    for r in range(slots):
        put(r, slice(width, width + kv), part[r * rank2 : (r + 1) * rank2])


def low_rank_call(place, tok, cot, packs, width, kv):
    slots = len(packs)
    rank2 = packs[0].shape[0]
    rows = tok.shape[0]
    half = struct((slots // 2, rank2, width + kv))
    return pl.pallas_call(
        functools.partial(low_rank_kernel, slots, rank2, width, kv),
        out_shape=(
            struct((rows, slots * rank2)),
            struct((rows, slots * rank2)),
            struct((slots * rank2, width)),
            struct((slots * rank2, kv)),
            half,
            half,
        ),
        in_specs=[SMEM] + [VMEM] * (2 + slots),
        out_specs=(VMEM,) * 6,
        compiler_params=params(),
        cost_estimate=COST,
        name="low_rank",
    )(place, tok, cot, *packs)


def matmul_kernel(plan, block, shard, rank2, kv, first, last, *refs):
    refs = list(refs)
    tok, cot, low, grad, down, up = (refs.pop(0) for _ in range(6))
    sources = [
        [refs.pop(0) if i is None else refs.pop(0).at[i] for i in picks] for picks, _, _ in plan
    ]
    if not first:
        acc_in = refs.pop(0)
        refs.pop(0)
    out, gx = refs.pop(0), refs.pop(0)
    stage, sems = refs.pop(0), refs.pop(0)
    acc = out
    if first:
        col = lax.broadcasted_iota(jnp.int32, low.shape, 1)
        is_key = (col % rank2) < (rank2 // 2)
        zero = jnp.zeros(low.shape, BF16)
        low_keys = jnp.where(is_key, low[...], zero)
        low_vals = jnp.where(is_key, zero, low[...])
        acc[:, :kv] = ADAPTER_SCALE * dot(low_keys, up[...])
        acc[:, kv:] = ADAPTER_SCALE * dot(low_vals, up[...])
    copies, pieces = [], []
    for (_, entry, total), chunks in zip(plan, sources):
        for at in range(0, total, block):
            number = len(pieces)
            offset = pl.multiple_of(weight_row(shard, *entry) + at, block)
            where = pl.ds(offset, block)
            back = dot(grad[...], down[:, where])
            start, parts = 0, []
            for chunk in chunks:
                cols = slice(start, start + chunk.shape[1])
                start += chunk.shape[1]
                parts.append((cols, chunk, at))
                back += dot(cot[:, cols], chunk[pl.ds(at, block), :], CONTRACT_LAST)
            stage[number] = back.astype(BF16)
            copy = pltpu.make_async_copy(stage.at[number], gx.at[:, where], sems.at[number])
            copy.start()
            copies.append(copy)
            pieces.append((where, parts))
    edges = sorted({cols.stop for _, parts in pieces for cols, _, _ in parts})
    for low_edge, edge in zip([0] + edges, edges):
        cols = slice(low_edge, edge)
        total = acc[:, cols] if first else acc_in[:, cols]
        for where, parts in pieces:
            span, chunk, at = next(p for p in parts if p[0].stop >= edge)
            inner = slice(low_edge - span.start, edge - span.start)
            total += dot(tok[:, where], chunk[pl.ds(at, block), inner])
        if last:
            out[:, cols] = total.astype(BF16)
        else:
            out[:, cols] = total
    for copy in copies:
        copy.wait()


def matmul_call(shard, tok, cot, low, grad, down, up, sources, prev, last, rank2, name):
    rows, width = tok.shape
    cols = cot.shape[1]
    kv = up.shape[1]
    sources = [
        (entry, [p if isinstance(p, tuple) else (p, None) for p in parts])
        for entry, parts in sources
    ]
    tall = [parts[0][0].shape[-2] for _, parts in sources]
    block = min(512, min(tall))
    plan = tuple(
        (tuple(i for _, i in parts), entry, total)
        for (entry, parts), total in zip(sources, tall)
    )
    flops = 4 * rows * cols * sum(total for _, _, total in plan)
    cost = pl.CostEstimate(flops=flops, bytes_accessed=1, transcendentals=0)
    count = sum(total // block for _, _, total in plan)
    arrays = [part for _, parts in sources for part, _ in parts]
    args = [tok, cot, low, grad, down, up] + arrays
    in_specs = [VMEM] * (6 + len(arrays))
    first = prev is None
    aliases = {}
    if not first:
        args += list(prev)
        in_specs += [VMEM, HBM]
        aliases = {len(args) - 1: 1}
        if not last:
            aliases[len(args) - 2] = 0
    scratch = [pltpu.VMEM((count, rows, block), BF16), pltpu.SemaphoreType.DMA((count,))]
    return pl.pallas_call(
        functools.partial(matmul_kernel, plan, block, shard, rank2, kv, first, last),
        out_shape=(struct((rows, cols), BF16 if last else F32), struct((rows, width))),
        in_specs=in_specs,
        out_specs=(VMEM, HBM),
        scratch_shapes=scratch,
        input_output_aliases=aliases,
        compiler_params=params(),
        cost_estimate=cost,
        name=name,
    )(*args)


def stack_kernel(*refs):
    for i, ref in enumerate(refs[:-1]):
        refs[-1][i] = ref[...]


def even_odd_kernel(keep, recv, even, odd):
    for i in range(even.shape[0]):
        for out, j in ((even, 2 * i), (odd, 2 * i + 1)):
            out[i] = (keep[j].astype(F32) + recv[j].astype(F32)).astype(BF16)


def halves_kernel(keep, recv, mine, other):
    half = mine.shape[0]
    parity = lax.axis_index("dp") % 2
    for out, upper in ((mine, parity), (other, 1 - parity)):
        row = pl.ds(pl.multiple_of(upper * half, half), half)
        out[...] = (keep[0, row, :].astype(F32) + recv[0, row, :].astype(F32)).astype(BF16)


def finish_kernel(width, mine, recv, down, up):
    half = mine.shape[0]
    parity = lax.axis_index("dp") % 2
    for part, upper in ((mine, parity), (recv, 1 - parity)):
        row = pl.ds(pl.multiple_of(upper * half, half), half)
        down[0, row, :] = part[:, :width].astype(F32)
        up[0, row, :] = part[:, width:].astype(F32)


def xor_swap(value, axis, size, bit):
    return lax.ppermute(value, axis, [(i, i ^ bit) for i in range(size)])


PREP_MIB = 54
SPANS = (7, 9)


def per_device(
    n_groups,
    n_dp,
    n_fsdp,
    tokens,
    key_value_weight,
    adapter_down_maps,
    adapter_up_maps,
    counts,
    tenant_slot_index,
    cotangent,
):
    rows, width = tokens.shape
    slots = tenant_slot_index.shape[0]
    rank2 = adapter_down_maps.shape[1]
    kv = adapter_up_maps.shape[2]
    shard = key_value_weight.shape[0]
    cols = key_value_weight.shape[1]
    swap = lambda value, bit: xor_swap(value, "fsdp", n_fsdp, bit)
    swap_y = lambda value: xor_swap(value, "groups", n_groups, 1)
    swap_z = lambda value: xor_swap(value, "dp", n_dp, 1)
    high_bits = [b for b in range(2, n_fsdp, 2)]
    quartered = n_groups == 2 and n_dp % 2 == 0 and n_fsdp == 4 and shard % 1024 == 0
    block = shard // 4
    place = jnp.concatenate([counts[0], tenant_slot_index])

    def local(kernel, outs, args, name, scratch=(), spaces=None, mib=16):
        spaces = spaces or [SMEM if a is place else VMEM for a in args]
        return pl.pallas_call(
            kernel,
            out_shape=tuple(outs),
            in_specs=spaces,
            out_specs=(VMEM,) * len(outs),
            scratch_shapes=list(scratch),
            compiler_params=params(mib),
            cost_estimate=COST,
            name=name,
        )(*args)

    barrier = lambda *values: lax.optimization_barrier(values)

    cuts, start = [], 0
    if quartered:
        for size in SPANS:
            cuts.append(((0, 0), start * cols // 16, size * cols // 16))
            start += size
        start = SPANS[0] * cols // 16
        cuts.append(((1, 1), start, cols - start))

    pack, *sent = local(
        functools.partial(pack_kernel, block, cuts[:1]),
        [struct((rank2, width + kv))] + [struct((block, size)) for _, _, size in cuts[:1]],
        (key_value_weight, adapter_down_maps, adapter_up_maps),
        "prep",
        [pltpu.SemaphoreType.DMA((2 + len(cuts[:1]),))],
        [HBM, HBM, HBM],
        PREP_MIB,
    )
    packs = {0: pack}
    for bit in high_bits + [1]:
        packs[bit] = swap(pack, bit)
    sibling = swap(key_value_weight, 1)
    if quartered:
        direct = [swap(sent[0], 2)]
        sent = list(sent) + list(
            local(
                functools.partial(prep_kernel, block, cuts[1:]),
                [struct((block, size)) for _, _, size in cuts[1:]],
                (key_value_weight,),
                "split",
                [pltpu.SemaphoreType.DMA((len(cuts) - 1,))],
                [HBM],
            )
        )
        first, second, *rest = sent
    loads = (tokens, cotangent, key_value_weight)
    tok, cot, weight = local(
        functools.partial(load_kernel, len(loads)),
        [struct(a.shape) for a in loads],
        loads,
        "load",
        [pltpu.SemaphoreType.DMA((len(loads),))],
        [HBM] * len(loads),
    )
    if quartered:
        packs[2], tok, second, sibling, *rest = barrier(
            packs[2], tok, second, sibling, *rest
        )
    for bit in high_bits:
        packs[bit], tok = barrier(packs[bit], tok)
        packs[bit + 1] = swap(packs[bit], 1)

    if quartered:
        direct[0], tok, packs[3] = barrier(direct[0], tok, packs[3])
    low, grad, down_cat, up_cat, keep, send = low_rank_call(
        place, tok, cot, [packs[r] for r in range(slots)], width, kv
    )

    def matmul(number, sources, prev, last=False):
        return matmul_call(
            shard,
            tok,
            cot,
            low,
            grad,
            down_cat,
            up_cat,
            sources,
            prev,
            last,
            rank2,
            f"matmul_{number}",
        )

    add = lambda a, b: (a.astype(F32) + b.astype(F32)).astype(BF16)
    half = struct((rank2 // 2, width + kv))
    finish = lambda mine, recv: local(
        functools.partial(finish_kernel, width),
        (struct((1, rank2, width), F32), struct((1, rank2, kv), F32)),
        (mine, recv),
        "finish",
    )
    recv = swap(send, 1)
    if not quartered:
        bit = 2
        while bit < n_fsdp:
            parts = struct((keep.shape[0] // 2,) + keep.shape[1:])
            keep, send = local(even_odd_kernel, (parts, parts), (keep, recv), "even_odd")
            recv = swap(send, bit)
            bit *= 2
        if n_dp == 1:
            total = add(keep[0], recv[0]).astype(F32)
            grad_down, grad_up = total[None, :, :width], total[None, :, width:]
        else:
            mine, other = local(halves_kernel, (half, half), (keep, recv), "halves")
            mine = add(mine, swap_z(other))
            bit = 2
            while bit < n_dp:
                mine = add(mine, xor_swap(mine, "dp", n_dp, bit))
                bit *= 2
            grad_down, grad_up = finish(mine, swap_z(mine))
        calls = [
            [((0, None), [weight])],
            [((1, None), [sibling])],
        ]
        for bit in high_bits:
            through = swap(key_value_weight, bit)
            calls.append(
                [
                    ((bit, None), [through]),
                    ((bit + 1, None), [swap(through, 1)]),
                ]
            )
        prev = None
        for number, sources in enumerate(calls):
            prev = matmul(number, sources, prev, number == len(calls) - 1)
        return prev[0], prev[1], grad_down, grad_up

    link = [keep]

    def after(*values):
        held = barrier(*values, *link)[: len(values)]
        link[:] = held[:1]
        return held if len(values) > 1 else held[0]

    def ready(values):
        held = after(*values)
        return list(held) if len(values) > 1 else [held]

    core = lambda parts: [swap(c, 1) for c in parts]
    parts = struct((1,) + keep.shape[1:])
    ahead = core(direct)
    via_y, via_z = [swap_y(direct[0])], [swap_z(direct[0])]
    keep, recv, ahead[0] = after(keep, recv, ahead[0])
    keep, send = local(even_odd_kernel, (parts, parts), (keep, recv), "even_odd")
    keep, send = after(keep, send)
    recv = swap(send, 2)
    low = after(low)
    prev = matmul(0, [((0, None), [weight])], None)
    rest = list(after(*sent[1:], *prev)[: len(sent) - 1])
    direct += [swap(c, 2) for c in rest[:-1]]
    across = swap(rest[-1], 2)
    recv, keep = after(recv, keep)
    mine, other = local(halves_kernel, (half, half), (keep, recv), "halves")
    mine, other = after(mine, other)
    recv = swap_z(other)
    via_z[0], via_y[0] = after(via_z[0], via_y[0])
    diagonal = [swap_y(via_z[0])]
    prev = after(*prev)
    prev = matmul(1, [((1, None), [sibling])], prev)
    prev = after(*prev)
    mine, recv = after(mine, recv)
    mine = after(add(mine, recv))
    bit = 2
    recv = xor_swap(mine, "dp", n_dp, bit) if n_dp > 2 else None
    for i in range(1, len(direct)):
        direct[i] = after(direct[i])
        via_y.append(swap_y(direct[i]))
        via_z.append(swap_z(direct[i]))
        if i == 1:
            diagonal[0] = after(diagonal[0])
    while bit < n_dp:
        if bit > 2:
            recv = xor_swap(mine, "dp", n_dp, bit)
        mine, recv = after(mine, recv)
        mine = after(add(mine, recv))
        bit *= 2
    other = swap_z(mine)

    ahead[1:] = ready(ahead[:1] + core(direct[1:]))[1:]
    early = (via_y[0], via_z[0], diagonal[0])
    (stacked,) = local(stack_kernel, (struct((3,) + early[0].shape),), early, "stack")
    stacked = after(stacked)
    crossed = swap(stacked, 1)
    prev = matmul(2, [((2, (0, 0)), direct), ((3, (0, 0)), ahead)], prev)
    prev = after(*prev)
    diagonal.append(after(across))
    prev = matmul(3, [((2, (1, 1)), diagonal)], prev)
    prev = after(*prev)
    via_y[1], via_z[1] = after(via_y[1], via_z[1])
    late = core((via_y[1], via_z[1], diagonal[1]))
    prev = matmul(4, [((2, (1, 0)), via_y), ((2, (0, 1)), via_z)], prev)
    keys = ((1, 0), (0, 1), (1, 1))
    sources = [((3, key), [(crossed, i), late[i]]) for i, key in enumerate(keys)]
    out, grad_x = matmul(5, sources, prev, True)
    out, mine, other = barrier(out, mine, other)
    grad_down, grad_up = finish(mine, other)
    return out, grad_x, grad_down, grad_up


def solution(mesh):
    in_specs = (
        P(("groups", "dp", "fsdp"), None),
        P("fsdp", None),
        P(("groups", "fsdp"), None, None),
        P(("groups", "fsdp"), None, None),
        P(("groups", "dp"), None),
        P("groups"),
        P(("groups", "dp", "fsdp"), None),
    )
    out_specs = (
        P(("groups", "dp", "fsdp"), None),
        P(("groups", "dp", "fsdp"), None),
        P(("groups", "fsdp"), None, None),
        P(("groups", "fsdp"), None, None),
    )
    body = functools.partial(
        per_device, mesh.shape["groups"], mesh.shape["dp"], mesh.shape["fsdp"]
    )
    return jax.shard_map(
        body, mesh=mesh, in_specs=in_specs, out_specs=out_specs, check_vma=False
    )
```

```python
import functools

import jax
import jax.numpy as jnp
from jax import lax
from jax.experimental import pallas as pl
from jax.experimental.pallas import tpu as pltpu
from jax.sharding import PartitionSpec as P

ADAPTER_SCALE = 2.0
F32 = jnp.float32
BF16 = jnp.bfloat16
CONTRACT_LAST = (((1,), (1,)), ((), ()))
CONTRACT_FIRST = (((0,), (0,)), ((), ()))
VMEM = pl.BlockSpec(memory_space=pltpu.VMEM)
SMEM = pl.BlockSpec(memory_space=pltpu.SMEM)
HBM = pl.BlockSpec(memory_space=pltpu.HBM)
COST = pl.CostEstimate(flops=1, bytes_accessed=1, transcendentals=0)


def params(mib=16):
    return pltpu.CompilerParams(vmem_limit_bytes=mib << 20)


def weight_row(shard, rel, key):
    me = lax.axis_index("fsdp")
    row = jnp.bitwise_xor(me, rel) * shard
    if key is not None:
        row = row + quarter_row(shard, key)
    return row


def quarter_row(shard, key):
    group, data = lax.axis_index("groups"), lax.axis_index("dp")
    a, b = key
    return (((group + a) % 2) * 2 + (data + b) % 2) * (shard // 4)


def dot(a, b, dims=(((1,), (0,)), ((), ()))):
    return lax.dot_general(a, b, dims, preferred_element_type=F32)


def struct(shape, dtype=BF16):
    return jax.ShapeDtypeStruct(shape, dtype)


def prep_kernel(block, cuts, weight, *refs):
    outs, sems = refs[: len(cuts)], refs[len(cuts)]
    copies = []
    for i, (key, start, span) in enumerate(cuts):
        row = pl.multiple_of(quarter_row(weight.shape[0], key), block)
        source = weight.at[pl.ds(row, block), pl.ds(start, span)]
        copies.append(pltpu.make_async_copy(source, outs[i], sems.at[i]))
    for copy in copies:
        copy.start()
    for copy in copies:
        copy.wait()


def pack_kernel(block, cuts, weight, down, up, pack, *refs):
    outs, sems = refs[: len(cuts)], refs[len(cuts)]
    width = down.shape[2]
    moves = [
        (down.at[0], pack.at[:, pl.ds(0, width)]),
        (up.at[0], pack.at[:, pl.ds(width, up.shape[2])]),
    ]
    for out, (key, start, span) in zip(outs, cuts):
        row = pl.multiple_of(quarter_row(weight.shape[0], key), block)
        moves.append((weight.at[pl.ds(row, block), pl.ds(start, span)], out))
    copies = [pltpu.make_async_copy(a, b, sems.at[i]) for i, (a, b) in enumerate(moves)]
    for copy in copies:
        copy.start()
    for copy in copies:
        copy.wait()


def load_kernel(count, *refs):
    sems = refs[2 * count]
    copies = [
        pltpu.make_async_copy(refs[i], refs[count + i], sems.at[i]) for i in range(count)
    ]
    for copy in copies:
        copy.start()
    for copy in copies:
        copy.wait()


def low_rank_kernel(slots, rank2, width, kv, place, tok, cot, *refs):
    packs = refs[:slots]
    spread_low, spread_grad, down_cat, up_cat, keep, send = refs[slots:]
    rows = tok.shape[0]
    me = lax.axis_index("fsdp")
    for r in range(slots):
        down_cat[pl.ds(r * rank2, rank2), :] = packs[r][:, :width]
        up_cat[pl.ds(r * rank2, rank2), :] = packs[r][:, width:]
    pos = me * rows + lax.broadcasted_iota(jnp.int32, (rows, slots * rank2), 0)
    col = lax.broadcasted_iota(jnp.int32, (rows, slots * rank2), 1)
    slot = col // rank2
    is_key = (col % rank2) < (rank2 // 2)
    own = jnp.full((rows, slots * rank2), -1, jnp.int32)
    start = jnp.int32(0)
    for u in range(slots):
        rel = jnp.bitwise_xor(place[slots + u], me)
        own = jnp.where(pos >= start, rel, own)
        start = start + place[u]
    mask = slot == own
    low = jnp.where(mask, dot(tok[...], down_cat[...], CONTRACT_LAST), 0.0).astype(BF16)
    spread_low[...] = low
    back_keys = dot(cot[:, :kv], up_cat[...], CONTRACT_LAST)
    back_vals = dot(cot[:, kv:], up_cat[...], CONTRACT_LAST)
    back = ADAPTER_SCALE * jnp.where(is_key, back_keys, back_vals)
    grad = jnp.where(mask, back, 0.0).astype(BF16)
    spread_grad[...] = grad

    def put(r, cols, value):
        ref = keep if r % 2 == 0 else send
        ref[r // 2, :, cols] = value.astype(BF16)

    step = 1024
    for start in range(0, width, step):
        part = dot(grad, tok[:, start : start + step], CONTRACT_FIRST)
        for r in range(slots):
            put(r, slice(start, start + step), part[r * rank2 : (r + 1) * rank2])
    part_keys = ADAPTER_SCALE * dot(low, cot[:, :kv], CONTRACT_FIRST)
    part_vals = ADAPTER_SCALE * dot(low, cot[:, kv:], CONTRACT_FIRST)
    row = lax.broadcasted_iota(jnp.int32, (slots * rank2, kv), 0)
    part = jnp.where((row % rank2) < (rank2 // 2), part_keys, part_vals)
    for r in range(slots):
        put(r, slice(width, width + kv), part[r * rank2 : (r + 1) * rank2])


def low_rank_call(place, tok, cot, packs, width, kv):
    slots = len(packs)
    rank2 = packs[0].shape[0]
    rows = tok.shape[0]
    half = struct((slots // 2, rank2, width + kv))
    return pl.pallas_call(
        functools.partial(low_rank_kernel, slots, rank2, width, kv),
        out_shape=(
            struct((rows, slots * rank2)),
            struct((rows, slots * rank2)),
            struct((slots * rank2, width)),
            struct((slots * rank2, kv)),
            half,
            half,
        ),
        in_specs=[SMEM] + [VMEM] * (2 + slots),
        out_specs=(VMEM,) * 6,
        compiler_params=params(),
        cost_estimate=COST,
        name="low_rank",
    )(place, tok, cot, *packs)


def matmul_kernel(plan, block, shard, rank2, kv, first, last, *refs):
    refs = list(refs)
    tok, cot, low, grad, down, up = (refs.pop(0) for _ in range(6))
    sources = [
        [refs.pop(0) if i is None else refs.pop(0).at[i] for i in picks] for picks, _, _ in plan
    ]
    if not first:
        acc_in = refs.pop(0)
        refs.pop(0)
    out, gx = refs.pop(0), refs.pop(0)
    stage, sems = refs.pop(0), refs.pop(0)
    held = refs.pop(0) if last else None
    acc = out
    if first:
        col = lax.broadcasted_iota(jnp.int32, low.shape, 1)
        is_key = (col % rank2) < (rank2 // 2)
        zero = jnp.zeros(low.shape, BF16)
        low_keys = jnp.where(is_key, low[...], zero)
        low_vals = jnp.where(is_key, zero, low[...])
        acc[:, :kv] = ADAPTER_SCALE * dot(low_keys, up[...])
        acc[:, kv:] = ADAPTER_SCALE * dot(low_vals, up[...])
    copies, pieces = [], []
    for (_, entry, total), chunks in zip(plan, sources):
        for at in range(0, total, block):
            number = len(pieces)
            offset = pl.multiple_of(weight_row(shard, *entry) + at, block)
            where = pl.ds(offset, block)
            back = dot(grad[...], down[:, where])
            start, parts = 0, []
            for chunk in chunks:
                cols = slice(start, start + chunk.shape[1])
                start += chunk.shape[1]
                parts.append((cols, chunk, at))
                back += dot(cot[:, cols], chunk[pl.ds(at, block), :], CONTRACT_LAST)
            stage[number] = back.astype(BF16)
            copy = pltpu.make_async_copy(stage.at[number], gx.at[:, where], sems.at[number])
            copy.start()
            copies.append(copy)
            pieces.append((where, parts))
    edges = sorted({cols.stop for _, parts in pieces for cols, _, _ in parts})
    for low_edge, edge in zip([0] + edges, edges):
        cols = slice(low_edge, edge)
        total = acc[:, cols] if first else acc_in[:, cols]
        for where, parts in pieces:
            span, chunk, at = next(p for p in parts if p[0].stop >= edge)
            inner = slice(low_edge - span.start, edge - span.start)
            total += dot(tok[:, where], chunk[pl.ds(at, block), inner])
        if last:
            number = len(copies)
            held[:, cols] = total.astype(BF16)
            copy = pltpu.make_async_copy(held.at[:, cols], out.at[:, cols], sems.at[number])
            copy.start()
            copies.append(copy)
        else:
            out[:, cols] = total
    for copy in copies:
        copy.wait()


def matmul_call(shard, tok, cot, low, grad, down, up, sources, prev, last, rank2, name):
    rows, width = tok.shape
    cols = cot.shape[1]
    kv = up.shape[1]
    sources = [
        (entry, [p if isinstance(p, tuple) else (p, None) for p in parts])
        for entry, parts in sources
    ]
    tall = [parts[0][0].shape[-2] for _, parts in sources]
    block = min(512, min(tall))
    plan = tuple(
        (tuple(i for _, i in parts), entry, total)
        for (entry, parts), total in zip(sources, tall)
    )
    flops = 4 * rows * cols * sum(total for _, _, total in plan)
    cost = pl.CostEstimate(flops=flops, bytes_accessed=1, transcendentals=0)
    count = sum(total // block for _, _, total in plan)
    arrays = [part for _, parts in sources for part, _ in parts]
    args = [tok, cot, low, grad, down, up] + arrays
    in_specs = [VMEM] * (6 + len(arrays))
    first = prev is None
    aliases = {}
    if not first:
        args += list(prev)
        in_specs += [VMEM, HBM]
        aliases = {len(args) - 1: 1}
        if not last:
            aliases[len(args) - 2] = 0
    widths = sum(len(parts) for _, parts in sources)
    sems = count + (widths if last else 0)
    scratch = [pltpu.VMEM((count, rows, block), BF16), pltpu.SemaphoreType.DMA((sems,))]
    if last:
        scratch.append(pltpu.VMEM((rows, cols), BF16))
    return pl.pallas_call(
        functools.partial(matmul_kernel, plan, block, shard, rank2, kv, first, last),
        out_shape=(struct((rows, cols), BF16 if last else F32), struct((rows, width))),
        in_specs=in_specs,
        out_specs=(HBM if last else VMEM, HBM),
        scratch_shapes=scratch,
        input_output_aliases=aliases,
        compiler_params=params(),
        cost_estimate=cost,
        name=name,
    )(*args)


def stack_kernel(*refs):
    for i, ref in enumerate(refs[:-1]):
        refs[-1][i] = ref[...]


def even_odd_kernel(keep, recv, even, odd):
    for i in range(even.shape[0]):
        for out, j in ((even, 2 * i), (odd, 2 * i + 1)):
            out[i] = (keep[j].astype(F32) + recv[j].astype(F32)).astype(BF16)


def halves_kernel(keep, recv, mine, other):
    half = mine.shape[0]
    parity = lax.axis_index("dp") % 2
    for out, upper in ((mine, parity), (other, 1 - parity)):
        row = pl.ds(pl.multiple_of(upper * half, half), half)
        out[...] = (keep[0, row, :].astype(F32) + recv[0, row, :].astype(F32)).astype(BF16)


def finish_kernel(width, mine, recv, down, up):
    half = mine.shape[0]
    parity = lax.axis_index("dp") % 2
    for part, upper in ((mine, parity), (recv, 1 - parity)):
        row = pl.ds(pl.multiple_of(upper * half, half), half)
        down[0, row, :] = part[:, :width].astype(F32)
        up[0, row, :] = part[:, width:].astype(F32)


def xor_swap(value, axis, size, bit):
    return lax.ppermute(value, axis, [(i, i ^ bit) for i in range(size)])


PREP_MIB = 54
SPANS = (7, 9)


def per_device(
    n_groups,
    n_dp,
    n_fsdp,
    tokens,
    key_value_weight,
    adapter_down_maps,
    adapter_up_maps,
    counts,
    tenant_slot_index,
    cotangent,
):
    rows, width = tokens.shape
    slots = tenant_slot_index.shape[0]
    rank2 = adapter_down_maps.shape[1]
    kv = adapter_up_maps.shape[2]
    shard = key_value_weight.shape[0]
    cols = key_value_weight.shape[1]
    swap = lambda value, bit: xor_swap(value, "fsdp", n_fsdp, bit)
    swap_y = lambda value: xor_swap(value, "groups", n_groups, 1)
    swap_z = lambda value: xor_swap(value, "dp", n_dp, 1)
    high_bits = [b for b in range(2, n_fsdp, 2)]
    quartered = n_groups == 2 and n_dp % 2 == 0 and n_fsdp == 4 and shard % 1024 == 0
    block = shard // 4
    place = jnp.concatenate([counts[0], tenant_slot_index])

    def local(kernel, outs, args, name, scratch=(), spaces=None, mib=16):
        spaces = spaces or [SMEM if a is place else VMEM for a in args]
        return pl.pallas_call(
            kernel,
            out_shape=tuple(outs),
            in_specs=spaces,
            out_specs=(VMEM,) * len(outs),
            scratch_shapes=list(scratch),
            compiler_params=params(mib),
            cost_estimate=COST,
            name=name,
        )(*args)

    barrier = lambda *values: lax.optimization_barrier(values)

    cuts, start = [], 0
    if quartered:
        for size in SPANS:
            cuts.append(((0, 0), start * cols // 16, size * cols // 16))
            start += size
        start = SPANS[0] * cols // 16
        cuts.append(((1, 1), start, cols - start))

    pack, *sent = local(
        functools.partial(pack_kernel, block, cuts[:1]),
        [struct((rank2, width + kv))] + [struct((block, size)) for _, _, size in cuts[:1]],
        (key_value_weight, adapter_down_maps, adapter_up_maps),
        "prep",
        [pltpu.SemaphoreType.DMA((2 + len(cuts[:1]),))],
        [HBM, HBM, HBM],
        PREP_MIB,
    )
    packs = {0: pack}
    for bit in high_bits + [1]:
        packs[bit] = swap(pack, bit)
    sibling = swap(key_value_weight, 1)
    if quartered:
        direct = [swap(sent[0], 2)]
        sent = list(sent) + list(
            local(
                functools.partial(prep_kernel, block, cuts[1:]),
                [struct((block, size)) for _, _, size in cuts[1:]],
                (key_value_weight,),
                "split",
                [pltpu.SemaphoreType.DMA((len(cuts) - 1,))],
                [HBM],
            )
        )
        first, second, *rest = sent
    loads = (tokens, cotangent, key_value_weight)
    tok, cot, weight = local(
        functools.partial(load_kernel, len(loads)),
        [struct(a.shape) for a in loads],
        loads,
        "load",
        [pltpu.SemaphoreType.DMA((len(loads),))],
        [HBM] * len(loads),
    )
    if quartered:
        packs[2], tok, second, sibling, *rest = barrier(
            packs[2], tok, second, sibling, *rest
        )
    for bit in high_bits:
        packs[bit], tok = barrier(packs[bit], tok)
        packs[bit + 1] = swap(packs[bit], 1)

    if quartered:
        direct[0], tok, packs[3] = barrier(direct[0], tok, packs[3])
    low, grad, down_cat, up_cat, keep, send = low_rank_call(
        place, tok, cot, [packs[r] for r in range(slots)], width, kv
    )

    def matmul(number, sources, prev, last=False):
        return matmul_call(
            shard,
            tok,
            cot,
            low,
            grad,
            down_cat,
            up_cat,
            sources,
            prev,
            last,
            rank2,
            f"matmul_{number}",
        )

    add = lambda a, b: (a.astype(F32) + b.astype(F32)).astype(BF16)
    half = struct((rank2 // 2, width + kv))
    finish = lambda mine, recv: local(
        functools.partial(finish_kernel, width),
        (struct((1, rank2, width), F32), struct((1, rank2, kv), F32)),
        (mine, recv),
        "finish",
    )
    recv = swap(send, 1)
    if not quartered:
        bit = 2
        while bit < n_fsdp:
            parts = struct((keep.shape[0] // 2,) + keep.shape[1:])
            keep, send = local(even_odd_kernel, (parts, parts), (keep, recv), "even_odd")
            recv = swap(send, bit)
            bit *= 2
        if n_dp == 1:
            total = add(keep[0], recv[0]).astype(F32)
            grad_down, grad_up = total[None, :, :width], total[None, :, width:]
        else:
            mine, other = local(halves_kernel, (half, half), (keep, recv), "halves")
            mine = add(mine, swap_z(other))
            bit = 2
            while bit < n_dp:
                mine = add(mine, xor_swap(mine, "dp", n_dp, bit))
                bit *= 2
            grad_down, grad_up = finish(mine, swap_z(mine))
        calls = [
            [((0, None), [weight])],
            [((1, None), [sibling])],
        ]
        for bit in high_bits:
            through = swap(key_value_weight, bit)
            calls.append(
                [
                    ((bit, None), [through]),
                    ((bit + 1, None), [swap(through, 1)]),
                ]
            )
        prev = None
        for number, sources in enumerate(calls):
            prev = matmul(number, sources, prev, number == len(calls) - 1)
        return prev[0], prev[1], grad_down, grad_up

    link = [keep]

    def after(*values):
        held = barrier(*values, *link)[: len(values)]
        link[:] = held[:1]
        return held if len(values) > 1 else held[0]

    def ready(values):
        held = after(*values)
        return list(held) if len(values) > 1 else [held]

    core = lambda parts: [swap(c, 1) for c in parts]
    parts = struct((1,) + keep.shape[1:])
    ahead = core(direct)
    via_y, via_z = [swap_y(direct[0])], [swap_z(direct[0])]
    keep, recv, ahead[0] = after(keep, recv, ahead[0])
    keep, send = local(even_odd_kernel, (parts, parts), (keep, recv), "even_odd")
    keep, send = after(keep, send)
    recv = swap(send, 2)
    low = after(low)
    prev = matmul(0, [((0, None), [weight])], None)
    rest = list(after(*sent[1:], *prev)[: len(sent) - 1])
    direct += [swap(c, 2) for c in rest[:-1]]
    across = swap(rest[-1], 2)
    recv, keep = after(recv, keep)
    mine, other = local(halves_kernel, (half, half), (keep, recv), "halves")
    mine, other = after(mine, other)
    recv = swap_z(other)
    via_z[0], via_y[0] = after(via_z[0], via_y[0])
    diagonal = [swap_y(via_z[0])]
    prev = after(*prev)
    prev = matmul(1, [((1, None), [sibling])], prev)
    prev = after(*prev)
    mine, recv = after(mine, recv)
    mine = after(add(mine, recv))
    bit = 2
    recv = xor_swap(mine, "dp", n_dp, bit) if n_dp > 2 else None
    for i in range(1, len(direct)):
        direct[i] = after(direct[i])
        via_y.append(swap_y(direct[i]))
        via_z.append(swap_z(direct[i]))
        if i == 1:
            diagonal[0] = after(diagonal[0])
    while bit < n_dp:
        if bit > 2:
            recv = xor_swap(mine, "dp", n_dp, bit)
        mine, recv = after(mine, recv)
        mine = after(add(mine, recv))
        bit *= 2
    other = swap_z(mine)

    ahead[1:] = ready(ahead[:1] + core(direct[1:]))[1:]
    early = (via_y[0], via_z[0], diagonal[0])
    (stacked,) = local(stack_kernel, (struct((3,) + early[0].shape),), early, "stack")
    stacked = after(stacked)
    crossed = swap(stacked, 1)
    prev = matmul(2, [((2, (0, 0)), direct), ((3, (0, 0)), ahead)], prev)
    prev = after(*prev)
    diagonal.append(after(across))
    prev = matmul(3, [((2, (1, 1)), diagonal)], prev)
    prev = after(*prev)
    via_y[1], via_z[1] = after(via_y[1], via_z[1])
    late = core((via_y[1], via_z[1], diagonal[1]))
    prev = matmul(4, [((2, (1, 0)), via_y), ((2, (0, 1)), via_z)], prev)
    keys = ((1, 0), (0, 1), (1, 1))
    sources = [((3, key), [(crossed, i), late[i]]) for i, key in enumerate(keys)]
    out, grad_x = matmul(5, sources, prev, True)
    out, mine, other = barrier(out, mine, other)
    grad_down, grad_up = finish(mine, other)
    return out, grad_x, grad_down, grad_up


def solution(mesh):
    in_specs = (
        P(("groups", "dp", "fsdp"), None),
        P("fsdp", None),
        P(("groups", "fsdp"), None, None),
        P(("groups", "fsdp"), None, None),
        P(("groups", "dp"), None),
        P("groups"),
        P(("groups", "dp", "fsdp"), None),
    )
    out_specs = (
        P(("groups", "dp", "fsdp"), None),
        P(("groups", "dp", "fsdp"), None),
        P(("groups", "fsdp"), None, None),
        P(("groups", "fsdp"), None, None),
    )
    body = functools.partial(
        per_device, mesh.shape["groups"], mesh.shape["dp"], mesh.shape["fsdp"]
    )
    return jax.shard_map(
        body, mesh=mesh, in_specs=in_specs, out_specs=out_specs, check_vma=False
    )
```

```python
import functools

import jax
import jax.numpy as jnp
from jax import lax
from jax.experimental import pallas as pl
from jax.experimental.pallas import tpu as pltpu
from jax.sharding import PartitionSpec as P

ADAPTER_SCALE = 2.0
F32 = jnp.float32
BF16 = jnp.bfloat16
CONTRACT_LAST = (((1,), (1,)), ((), ()))
CONTRACT_FIRST = (((0,), (0,)), ((), ()))
VMEM = pl.BlockSpec(memory_space=pltpu.VMEM)
SMEM = pl.BlockSpec(memory_space=pltpu.SMEM)
HBM = pl.BlockSpec(memory_space=pltpu.HBM)
COST = pl.CostEstimate(flops=1, bytes_accessed=1, transcendentals=0)


def params(mib=16):
    return pltpu.CompilerParams(vmem_limit_bytes=mib << 20)


def weight_row(shard, rel, key):
    me = lax.axis_index("fsdp")
    row = jnp.bitwise_xor(me, rel) * shard
    if key is not None:
        row = row + quarter_row(shard, key)
    return row


def quarter_row(shard, key):
    group, data = lax.axis_index("groups"), lax.axis_index("dp")
    a, b = key
    return (((group + a) % 2) * 2 + (data + b) % 2) * (shard // 4)


def dot(a, b, dims=(((1,), (0,)), ((), ()))):
    return lax.dot_general(a, b, dims, preferred_element_type=F32)


def struct(shape, dtype=BF16):
    return jax.ShapeDtypeStruct(shape, dtype)


def prep_kernel(block, cuts, weight, *refs):
    outs, sems = refs[: len(cuts)], refs[len(cuts)]
    copies = []
    for i, (key, start, span) in enumerate(cuts):
        row = pl.multiple_of(quarter_row(weight.shape[0], key), block)
        source = weight.at[pl.ds(row, block), pl.ds(start, span)]
        copies.append(pltpu.make_async_copy(source, outs[i], sems.at[i]))
    for copy in copies:
        copy.start()
    for copy in copies:
        copy.wait()


def pack_kernel(block, cuts, weight, down, up, pack, *refs):
    outs, sems = refs[: len(cuts)], refs[len(cuts)]
    width = down.shape[2]
    moves = [
        (down.at[0], pack.at[:, pl.ds(0, width)]),
        (up.at[0], pack.at[:, pl.ds(width, up.shape[2])]),
    ]
    for out, (key, start, span) in zip(outs, cuts):
        row = pl.multiple_of(quarter_row(weight.shape[0], key), block)
        moves.append((weight.at[pl.ds(row, block), pl.ds(start, span)], out))
    copies = [pltpu.make_async_copy(a, b, sems.at[i]) for i, (a, b) in enumerate(moves)]
    for copy in copies:
        copy.start()
    for copy in copies:
        copy.wait()


def load_kernel(count, *refs):
    sems = refs[2 * count]
    copies = [
        pltpu.make_async_copy(refs[i], refs[count + i], sems.at[i]) for i in range(count)
    ]
    for copy in copies:
        copy.start()
    for copy in copies:
        copy.wait()


def low_rank_kernel(slots, rank2, width, kv, place, tok, cot, *refs):
    packs = refs[:slots]
    spread_low, spread_grad, down_cat, up_cat, keep, send = refs[slots:]
    rows = tok.shape[0]
    me = lax.axis_index("fsdp")
    for r in range(slots):
        down_cat[pl.ds(r * rank2, rank2), :] = packs[r][:, :width]
        up_cat[pl.ds(r * rank2, rank2), :] = packs[r][:, width:]
    pos = me * rows + lax.broadcasted_iota(jnp.int32, (rows, slots * rank2), 0)
    col = lax.broadcasted_iota(jnp.int32, (rows, slots * rank2), 1)
    slot = col // rank2
    is_key = (col % rank2) < (rank2 // 2)
    own = jnp.full((rows, slots * rank2), -1, jnp.int32)
    start = jnp.int32(0)
    for u in range(slots):
        rel = jnp.bitwise_xor(place[slots + u], me)
        own = jnp.where(pos >= start, rel, own)
        start = start + place[u]
    mask = slot == own
    low = jnp.where(mask, dot(tok[...], down_cat[...], CONTRACT_LAST), 0.0).astype(BF16)
    spread_low[...] = low
    back_keys = dot(cot[:, :kv], up_cat[...], CONTRACT_LAST)
    back_vals = dot(cot[:, kv:], up_cat[...], CONTRACT_LAST)
    back = ADAPTER_SCALE * jnp.where(is_key, back_keys, back_vals)
    grad = jnp.where(mask, back, 0.0).astype(BF16)
    spread_grad[...] = grad

    def put(r, cols, value):
        ref = keep if r % 2 == 0 else send
        ref[r // 2, :, cols] = value.astype(BF16)

    step = 1024
    for start in range(0, width, step):
        part = dot(grad, tok[:, start : start + step], CONTRACT_FIRST)
        for r in range(slots):
            put(r, slice(start, start + step), part[r * rank2 : (r + 1) * rank2])
    part_keys = ADAPTER_SCALE * dot(low, cot[:, :kv], CONTRACT_FIRST)
    part_vals = ADAPTER_SCALE * dot(low, cot[:, kv:], CONTRACT_FIRST)
    row = lax.broadcasted_iota(jnp.int32, (slots * rank2, kv), 0)
    part = jnp.where((row % rank2) < (rank2 // 2), part_keys, part_vals)
    for r in range(slots):
        put(r, slice(width, width + kv), part[r * rank2 : (r + 1) * rank2])


def low_rank_call(place, tok, cot, packs, width, kv):
    slots = len(packs)
    rank2 = packs[0].shape[0]
    rows = tok.shape[0]
    half = struct((slots // 2, rank2, width + kv))
    return pl.pallas_call(
        functools.partial(low_rank_kernel, slots, rank2, width, kv),
        out_shape=(
            struct((rows, slots * rank2)),
            struct((rows, slots * rank2)),
            struct((slots * rank2, width)),
            struct((slots * rank2, kv)),
            half,
            half,
        ),
        in_specs=[SMEM] + [VMEM] * (2 + slots),
        out_specs=(VMEM,) * 6,
        compiler_params=params(),
        cost_estimate=COST,
        name="low_rank",
    )(place, tok, cot, *packs)


def matmul_kernel(plan, block, shard, rank2, kv, first, last, *refs):
    refs = list(refs)
    tok, cot, low, grad, down, up = (refs.pop(0) for _ in range(6))
    sources = [
        [refs.pop(0) if i is None else refs.pop(0).at[i] for i in picks] for picks, _, _ in plan
    ]
    if not first:
        acc_in = refs.pop(0)
        refs.pop(0)
    out, gx = refs.pop(0), refs.pop(0)
    stage, sems = refs.pop(0), refs.pop(0)
    held = refs.pop(0) if last else None
    acc = out
    if first:
        col = lax.broadcasted_iota(jnp.int32, low.shape, 1)
        is_key = (col % rank2) < (rank2 // 2)
        zero = jnp.zeros(low.shape, BF16)
        low_keys = jnp.where(is_key, low[...], zero)
        low_vals = jnp.where(is_key, zero, low[...])
        acc[:, :kv] = ADAPTER_SCALE * dot(low_keys, up[...])
        acc[:, kv:] = ADAPTER_SCALE * dot(low_vals, up[...])
    copies, pieces = [], []
    for (_, entry, total), chunks in zip(plan, sources):
        for at in range(0, total, block):
            number = len(pieces)
            offset = pl.multiple_of(weight_row(shard, *entry) + at, block)
            where = pl.ds(offset, block)
            back = dot(grad[...], down[:, where])
            start, parts = 0, []
            for chunk in chunks:
                cols = slice(start, start + chunk.shape[1])
                start += chunk.shape[1]
                parts.append((cols, chunk, at))
                back += dot(cot[:, cols], chunk[pl.ds(at, block), :], CONTRACT_LAST)
            stage[number] = back.astype(BF16)
            copy = pltpu.make_async_copy(stage.at[number], gx.at[:, where], sems.at[number])
            copy.start()
            copies.append(copy)
            pieces.append((where, parts))
    edges = sorted({cols.stop for _, parts in pieces for cols, _, _ in parts})
    for low_edge, edge in zip([0] + edges, edges):
        cols = slice(low_edge, edge)
        total = acc[:, cols] if first else acc_in[:, cols]
        for where, parts in pieces:
            span, chunk, at = next(p for p in parts if p[0].stop >= edge)
            inner = slice(low_edge - span.start, edge - span.start)
            total += dot(tok[:, where], chunk[pl.ds(at, block), inner])
        if last:
            number = len(copies)
            held[:, cols] = total.astype(BF16)
            copy = pltpu.make_async_copy(held.at[:, cols], out.at[:, cols], sems.at[number])
            copy.start()
            copies.append(copy)
        else:
            out[:, cols] = total
    for copy in copies:
        copy.wait()


def matmul_call(shard, tok, cot, low, grad, down, up, sources, prev, last, rank2, name):
    rows, width = tok.shape
    cols = cot.shape[1]
    kv = up.shape[1]
    sources = [
        (entry, [p if isinstance(p, tuple) else (p, None) for p in parts])
        for entry, parts in sources
    ]
    tall = [parts[0][0].shape[-2] for _, parts in sources]
    block = min(512, min(tall))
    plan = tuple(
        (tuple(i for _, i in parts), entry, total)
        for (entry, parts), total in zip(sources, tall)
    )
    flops = 4 * rows * cols * sum(total for _, _, total in plan)
    cost = pl.CostEstimate(flops=flops, bytes_accessed=1, transcendentals=0)
    count = sum(total // block for _, _, total in plan)
    arrays = [part for _, parts in sources for part, _ in parts]
    args = [tok, cot, low, grad, down, up] + arrays
    in_specs = [VMEM] * (6 + len(arrays))
    first = prev is None
    aliases = {}
    if not first:
        args += list(prev)
        in_specs += [VMEM, HBM]
        aliases = {len(args) - 1: 1}
        if not last:
            aliases[len(args) - 2] = 0
    widths = sum(len(parts) for _, parts in sources)
    sems = count + (widths if last else 0)
    scratch = [pltpu.VMEM((count, rows, block), BF16), pltpu.SemaphoreType.DMA((sems,))]
    if last:
        scratch.append(pltpu.VMEM((rows, cols), BF16))
    return pl.pallas_call(
        functools.partial(matmul_kernel, plan, block, shard, rank2, kv, first, last),
        out_shape=(struct((rows, cols), BF16 if last else F32), struct((rows, width))),
        in_specs=in_specs,
        out_specs=(HBM if last else VMEM, HBM),
        scratch_shapes=scratch,
        input_output_aliases=aliases,
        compiler_params=params(),
        cost_estimate=cost,
        name=name,
    )(*args)


def stack_kernel(*refs):
    for i, ref in enumerate(refs[:-1]):
        refs[-1][i] = ref[...]


def even_odd_kernel(keep, recv, even, odd):
    for i in range(even.shape[0]):
        for out, j in ((even, 2 * i), (odd, 2 * i + 1)):
            out[i] = (keep[j].astype(F32) + recv[j].astype(F32)).astype(BF16)


def halves_kernel(keep, recv, mine, other):
    half = mine.shape[0]
    parity = lax.axis_index("dp") % 2
    for out, upper in ((mine, parity), (other, 1 - parity)):
        row = pl.ds(pl.multiple_of(upper * half, half), half)
        out[...] = (keep[0, row, :].astype(F32) + recv[0, row, :].astype(F32)).astype(BF16)


def finish_kernel(width, mine, recv, down, up):
    half = mine.shape[0]
    parity = lax.axis_index("dp") % 2
    for part, upper in ((mine, parity), (recv, 1 - parity)):
        row = pl.ds(pl.multiple_of(upper * half, half), half)
        down[0, row, :] = part[:, :width].astype(F32)
        up[0, row, :] = part[:, width:].astype(F32)


def xor_swap(value, axis, size, bit):
    return lax.ppermute(value, axis, [(i, i ^ bit) for i in range(size)])


PREP_MIB = 54
SPANS = (8, 8)


def per_device(
    n_groups,
    n_dp,
    n_fsdp,
    tokens,
    key_value_weight,
    adapter_down_maps,
    adapter_up_maps,
    counts,
    tenant_slot_index,
    cotangent,
):
    rows, width = tokens.shape
    slots = tenant_slot_index.shape[0]
    rank2 = adapter_down_maps.shape[1]
    kv = adapter_up_maps.shape[2]
    shard = key_value_weight.shape[0]
    cols = key_value_weight.shape[1]
    swap = lambda value, bit: xor_swap(value, "fsdp", n_fsdp, bit)
    swap_y = lambda value: xor_swap(value, "groups", n_groups, 1)
    swap_z = lambda value: xor_swap(value, "dp", n_dp, 1)
    high_bits = [b for b in range(2, n_fsdp, 2)]
    quartered = n_groups == 2 and n_dp % 2 == 0 and n_fsdp == 4 and shard % 1024 == 0
    block = shard // 4
    place = jnp.concatenate([counts[0], tenant_slot_index])

    def local(kernel, outs, args, name, scratch=(), spaces=None, mib=16):
        spaces = spaces or [SMEM if a is place else VMEM for a in args]
        return pl.pallas_call(
            kernel,
            out_shape=tuple(outs),
            in_specs=spaces,
            out_specs=(VMEM,) * len(outs),
            scratch_shapes=list(scratch),
            compiler_params=params(mib),
            cost_estimate=COST,
            name=name,
        )(*args)

    barrier = lambda *values: lax.optimization_barrier(values)

    cuts, start = [], 0
    if quartered:
        for size in SPANS:
            cuts.append(((0, 0), start * cols // 16, size * cols // 16))
            start += size
        start = SPANS[0] * cols // 16
        cuts.append(((1, 1), start, cols - start))

    pack, *sent = local(
        functools.partial(pack_kernel, block, cuts[:1]),
        [struct((rank2, width + kv))] + [struct((block, size)) for _, _, size in cuts[:1]],
        (key_value_weight, adapter_down_maps, adapter_up_maps),
        "prep",
        [pltpu.SemaphoreType.DMA((2 + len(cuts[:1]),))],
        [HBM, HBM, HBM],
        PREP_MIB,
    )
    packs = {0: pack}
    for bit in high_bits + [1]:
        packs[bit] = swap(pack, bit)
    sibling = swap(key_value_weight, 1)
    if quartered:
        direct = [swap(sent[0], 2)]
        sent = list(sent) + list(
            local(
                functools.partial(prep_kernel, block, cuts[1:]),
                [struct((block, size)) for _, _, size in cuts[1:]],
                (key_value_weight,),
                "split",
                [pltpu.SemaphoreType.DMA((len(cuts) - 1,))],
                [HBM],
            )
        )
        first, second, *rest = sent
    loads = (tokens, cotangent, key_value_weight)
    tok, cot, weight = local(
        functools.partial(load_kernel, len(loads)),
        [struct(a.shape) for a in loads],
        loads,
        "load",
        [pltpu.SemaphoreType.DMA((len(loads),))],
        [HBM] * len(loads),
    )
    if quartered:
        packs[2], tok, second, sibling, *rest = barrier(
            packs[2], tok, second, sibling, *rest
        )
    for bit in high_bits:
        packs[bit], tok = barrier(packs[bit], tok)
        packs[bit + 1] = swap(packs[bit], 1)

    if quartered:
        direct[0], tok, packs[3] = barrier(direct[0], tok, packs[3])
    low, grad, down_cat, up_cat, keep, send = low_rank_call(
        place, tok, cot, [packs[r] for r in range(slots)], width, kv
    )

    def matmul(number, sources, prev, last=False):
        return matmul_call(
            shard,
            tok,
            cot,
            low,
            grad,
            down_cat,
            up_cat,
            sources,
            prev,
            last,
            rank2,
            f"matmul_{number}",
        )

    add = lambda a, b: (a.astype(F32) + b.astype(F32)).astype(BF16)
    half = struct((rank2 // 2, width + kv))
    finish = lambda mine, recv: local(
        functools.partial(finish_kernel, width),
        (struct((1, rank2, width), F32), struct((1, rank2, kv), F32)),
        (mine, recv),
        "finish",
    )
    recv = swap(send, 1)
    if not quartered:
        bit = 2
        while bit < n_fsdp:
            parts = struct((keep.shape[0] // 2,) + keep.shape[1:])
            keep, send = local(even_odd_kernel, (parts, parts), (keep, recv), "even_odd")
            recv = swap(send, bit)
            bit *= 2
        if n_dp == 1:
            total = add(keep[0], recv[0]).astype(F32)
            grad_down, grad_up = total[None, :, :width], total[None, :, width:]
        else:
            mine, other = local(halves_kernel, (half, half), (keep, recv), "halves")
            mine = add(mine, swap_z(other))
            bit = 2
            while bit < n_dp:
                mine = add(mine, xor_swap(mine, "dp", n_dp, bit))
                bit *= 2
            grad_down, grad_up = finish(mine, swap_z(mine))
        calls = [
            [((0, None), [weight])],
            [((1, None), [sibling])],
        ]
        for bit in high_bits:
            through = swap(key_value_weight, bit)
            calls.append(
                [
                    ((bit, None), [through]),
                    ((bit + 1, None), [swap(through, 1)]),
                ]
            )
        prev = None
        for number, sources in enumerate(calls):
            prev = matmul(number, sources, prev, number == len(calls) - 1)
        return prev[0], prev[1], grad_down, grad_up

    link = [keep]

    def after(*values):
        held = barrier(*values, *link)[: len(values)]
        link[:] = held[:1]
        return held if len(values) > 1 else held[0]

    def ready(values):
        held = after(*values)
        return list(held) if len(values) > 1 else [held]

    core = lambda parts: [swap(c, 1) for c in parts]
    parts = struct((1,) + keep.shape[1:])
    ahead = core(direct)
    via_y, via_z = [swap_y(direct[0])], [swap_z(direct[0])]
    keep, recv, ahead[0] = after(keep, recv, ahead[0])
    keep, send = local(even_odd_kernel, (parts, parts), (keep, recv), "even_odd")
    keep, send = after(keep, send)
    recv = swap(send, 2)
    low = after(low)
    prev = matmul(0, [((0, None), [weight])], None)
    rest = list(after(*sent[1:], *prev)[: len(sent) - 1])
    direct += [swap(c, 2) for c in rest[:-1]]
    across = swap(rest[-1], 2)
    recv, keep = after(recv, keep)
    mine, other = local(halves_kernel, (half, half), (keep, recv), "halves")
    mine, other = after(mine, other)
    recv = swap_z(other)
    via_z[0], via_y[0] = after(via_z[0], via_y[0])
    diagonal = [swap_y(via_z[0])]
    prev = after(*prev)
    prev = matmul(1, [((1, None), [sibling])], prev)
    prev = after(*prev)
    mine, recv = after(mine, recv)
    mine = after(add(mine, recv))
    bit = 2
    recv = xor_swap(mine, "dp", n_dp, bit) if n_dp > 2 else None
    for i in range(1, len(direct)):
        direct[i] = after(direct[i])
        via_y.append(swap_y(direct[i]))
        via_z.append(swap_z(direct[i]))
        if i == 1:
            diagonal[0] = after(diagonal[0])
    while bit < n_dp:
        if bit > 2:
            recv = xor_swap(mine, "dp", n_dp, bit)
        mine, recv = after(mine, recv)
        mine = after(add(mine, recv))
        bit *= 2
    other = swap_z(mine)

    ahead[1:] = ready(ahead[:1] + core(direct[1:]))[1:]
    early = (via_y[0], via_z[0], diagonal[0])
    (stacked,) = local(stack_kernel, (struct((3,) + early[0].shape),), early, "stack")
    stacked = after(stacked)
    crossed = swap(stacked, 1)
    prev = matmul(2, [((2, (0, 0)), direct), ((3, (0, 0)), ahead)], prev)
    prev = after(*prev)
    diagonal.append(after(across))
    prev = matmul(3, [((2, (1, 1)), diagonal)], prev)
    prev = after(*prev)
    via_y[1], via_z[1] = after(via_y[1], via_z[1])
    late = core((via_y[1], via_z[1], diagonal[1]))
    prev = matmul(4, [((2, (1, 0)), via_y), ((2, (0, 1)), via_z)], prev)
    keys = ((1, 0), (0, 1), (1, 1))
    sources = [((3, key), [(crossed, i), late[i]]) for i, key in enumerate(keys)]
    out, grad_x = matmul(5, sources, prev, True)
    out, mine, other = barrier(out, mine, other)
    grad_down, grad_up = finish(mine, other)
    return out, grad_x, grad_down, grad_up


def solution(mesh):
    in_specs = (
        P(("groups", "dp", "fsdp"), None),
        P("fsdp", None),
        P(("groups", "fsdp"), None, None),
        P(("groups", "fsdp"), None, None),
        P(("groups", "dp"), None),
        P("groups"),
        P(("groups", "dp", "fsdp"), None),
    )
    out_specs = (
        P(("groups", "dp", "fsdp"), None),
        P(("groups", "dp", "fsdp"), None),
        P(("groups", "fsdp"), None, None),
        P(("groups", "fsdp"), None, None),
    )
    body = functools.partial(
        per_device, mesh.shape["groups"], mesh.shape["dp"], mesh.shape["fsdp"]
    )
    return jax.shard_map(
        body, mesh=mesh, in_specs=in_specs, out_specs=out_specs, check_vma=False
    )
```
